32 devices in a mesh: batch: 8 (over z, x), row: 2 (over y), col: 2 (over core).
Axes of the slice: x: 2, y: 2, z: 4, core: 2. Of those that a mesh axis runs over, the one named last changes fastest.
Arguments:
- patches: float32 [8, 2, 2, 16, 256], P('batch', 'row', 'col'), may hold values from -6 to 6
- cond: float32 [8, 4, 384], P('batch'), may hold values from -6 to 6
- image_lengths: int32 [8, 1, 4], P('batch'), may hold values from 0 to 1024, as said below
- cotangent: float32 [8, 2, 2, 32, 256], P('batch', 'row', 'col'), may hold values from -6 to 6
- w_patch: float32 [16, 384], replicated, may hold values from -1.5 to 1.5
- b_patch: float32 [384], replicated, may hold values from -1.75 to 1.75
- w_mod: float32 [384, 2304], replicated, may hold values from -0.3125 to 0.3125
- b_mod: float32 [2304], replicated, may hold values from -1.75 to 1.75
- w_qkv: float32 [384, 1152], replicated, may hold values from -0.3125 to 0.3125
- b_query: float32 [384], replicated, may hold values from -1.75 to 1.75
- b_value: float32 [384], replicated, may hold values from -1.75 to 1.75
- w_proj: float32 [384, 384], replicated, may hold values from -1.75 to 1.75
- b_proj: float32 [384], replicated, may hold values from -1.75 to 1.75
- w_fc1: float32 [384, 1536], replicated, may hold values from -0.3125 to 0.3125
- b_fc1: float32 [1536], replicated, may hold values from -1.75 to 1.75
- w_fc2: float32 [1536, 384], replicated, may hold values from -0.15625 to 0.15625
- b_fc2: float32 [384], replicated, may hold values from -1.75 to 1.75
- w_fmod: float32 [384, 768], replicated, may hold values from -0.3125 to 0.3125
- b_fmod: float32 [768], replicated, may hold values from -1.75 to 1.75
- w_out: float32 [384, 32], replicated, may hold values from -0.3125 to 0.3125
- b_out: float32 [32], replicated, may hold values from -1.75 to 1.75
Outputs:
- output: float32 [8, 2, 2, 32, 256], P('batch', 'row', 'col')
- grad_patches: float32 [8, 2, 2, 16, 256], P('batch', 'row', 'col')
- grad_cond: float32 [8, 4, 384], P('batch')
- grad_w_patch: float32 [16, 384], replicated
- grad_b_patch: float32 [384], replicated
- grad_w_mod: float32 [384, 2304], replicated
- grad_b_mod: float32 [2304], replicated
- grad_w_qkv: float32 [384, 1152], replicated
- grad_b_query: float32 [384], replicated
- grad_b_value: float32 [384], replicated
- grad_w_proj: float32 [384, 384], replicated
- grad_b_proj: float32 [384], replicated
- grad_w_fc1: float32 [384, 1536], replicated
- grad_b_fc1: float32 [1536], replicated
- grad_w_fc2: float32 [1536, 384], replicated
- grad_b_fc2: float32 [384], replicated
- grad_w_fmod: float32 [384, 768], replicated
- grad_b_fmod: float32 [768], replicated
- grad_w_out: float32 [384, 32], replicated
- grad_b_out: float32 [32], replicated
The draws below stay inside these ranges and needn't reach their ends.
Inputs may be any that keep to these rules, and one draw needn't show every extreme that they name: `image_lengths`: each pack holds either one image of 1024 tokens followed by empty slots of length 0, or 4 images of 256 tokens; the lengths of a pack add up to 1024.
All inputs are finite; a program needn't handle non-finite values.
Results may differ from the reference program's by a relative error of at most 0.012.
The reference program's roundings to bfloat16 on the way count: a program that leaves them out, or rounds other values in their place, can miss the bound.
Values may be sent and summed in bfloat16 or wider, within the bound.
No kernel may reach another device: no remote copies, remote signals or barrier semaphores. Data moves between devices by JAX's collectives and lax.ppermute only.
A program may use at most 128 MiB of HBM per device.

```python
import math
import jax
import jax.numpy as jnp
from jax import lax

D = 384
HEADS = 6
HEAD_DIM = 64
FF = 1536
PATCH_IN = 16
OUT_CH = 32
BIG_SIDE = 16
SMALL_SIDE = 8
NPACK = 1
GROUPS = 8
ROWS = 2
COLS = 2
BIG_LEN = 1024
SMALL_LEN = 256
PACK = 1024
IMGS = 4
PT = 256
TOK_DEV = 256
SLOTS = 4


def draw_image_lengths(key, part):
    big_count = jax.random.randint(key, (GROUPS, NPACK), 0, 2).astype(jnp.int32)
    first_pack = (jnp.arange(GROUPS, dtype=jnp.int32)[:, None] == 0) & (jnp.arange(NPACK, dtype=jnp.int32)[None, :] == 0)
    big_count = jnp.where(first_pack, 1, big_count).astype(jnp.int32)
    small_count = ((PACK - BIG_LEN * big_count) // SMALL_LEN).astype(jnp.int32)
    slot_index = jnp.arange(IMGS, dtype=jnp.int32)[None, None, :]
    lengths = jnp.where(slot_index < big_count[:, :, None], BIG_LEN, jnp.where(slot_index < (big_count + small_count)[:, :, None], SMALL_LEN, 0))
    return lengths.astype(jnp.int32)


def block_levels(rng, extent, pieces, smallest, high):
    factor_of = 1.0
    for dim, shards_of in pieces:
        draws = jax.random.uniform(jax.random.fold_in(jax.random.fold_in(rng, 6), dim), (shards_of,), jnp.float32, smallest / len(pieces), high / len(pieces))
        factor_of = factor_of * jnp.repeat(jnp.exp(draws), extent[dim] // shards_of).reshape((-1,) + (1,) * (len(extent) - 1 - dim))
    return factor_of


def normal_values(key, shape, scale, reach, cuts=(), kind=jnp.bfloat16):
    values = scale * jax.random.normal(key, shape, jnp.float32)
    if cuts:
        values = values * block_levels(key, shape, cuts, -0.22, 0.18)
    return jnp.clip(values, -reach, reach).astype(kind)


def setup_inputs(seed: int = 0) -> dict:
    streams_of = jax.random.split(jax.random.key(seed), 22)
    return {
        "patches": normal_values(streams_of[0], (GROUPS, ROWS, COLS, PATCH_IN, TOK_DEV), 1.0, 6.0, ((0, 8), (1, 2), (2, 2)), jnp.float32),
        "cond": normal_values(streams_of[1], (GROUPS, SLOTS, D), 1.0, 6.0, ((0, 8),), jnp.float32),
        "image_lengths": draw_image_lengths(jax.random.fold_in(streams_of[21], 71), 0),
        "cotangent": normal_values(streams_of[3], (GROUPS, ROWS, COLS, OUT_CH, TOK_DEV), 1.0, 6.0, ((0, 8), (1, 2), (2, 2)), jnp.float32),
        "w_patch": normal_values(streams_of[4], (PATCH_IN, D), PATCH_IN ** -0.5, 1.5, (), jnp.float32),
        "b_patch": normal_values(streams_of[5], (D,), 0.3, 1.75, (), jnp.float32),
        "w_mod": normal_values(streams_of[6], (D, 6 * D), D ** -0.5, 0.3125, (), jnp.float32),
        "b_mod": normal_values(streams_of[7], (6 * D,), 0.3, 1.75, (), jnp.float32),
        "w_qkv": normal_values(streams_of[8], (D, 3 * D), D ** -0.5, 0.3125, (), jnp.float32),
        "b_query": normal_values(streams_of[9], (D,), 0.3, 1.75, (), jnp.float32),
        "b_value": normal_values(streams_of[10], (D,), 0.3, 1.75, (), jnp.float32),
        "w_proj": normal_values(streams_of[11], (D, D), (D // 32) ** -0.5, 1.75, (), jnp.float32),
        "b_proj": normal_values(streams_of[12], (D,), 0.3, 1.75, (), jnp.float32),
        "w_fc1": normal_values(streams_of[13], (D, FF), D ** -0.5, 0.3125, (), jnp.float32),
        "b_fc1": normal_values(streams_of[14], (FF,), 0.3, 1.75, (), jnp.float32),
        "w_fc2": normal_values(streams_of[15], (FF, D), FF ** -0.5, 0.15625, (), jnp.float32),
        "b_fc2": normal_values(streams_of[16], (D,), 0.3, 1.75, (), jnp.float32),
        "w_fmod": normal_values(streams_of[17], (D, 2 * D), D ** -0.5, 0.3125, (), jnp.float32),
        "b_fmod": normal_values(streams_of[18], (2 * D,), 0.3, 1.75, (), jnp.float32),
        "w_out": normal_values(streams_of[19], (D, OUT_CH), D ** -0.5, 0.3125, (), jnp.float32),
        "b_out": normal_values(streams_of[20], (OUT_CH,), 0.3, 1.75, (), jnp.float32),
    }


@jax.custom_vjp
def low(v):
    return lax.optimization_barrier(v.astype(jnp.bfloat16)).astype(jnp.float32)

@jax.custom_vjp
def low_back(v):
    return v

def low_keep(v):
    return (low(v), None)

def low_pass(kept, grad):
    return (grad,)

def back_keep(v):
    return (v, None)

def back_low(kept, grad):
    return (low(grad),)
low.defvjp(low_keep, low_pass)
low_back.defvjp(back_keep, back_low)
exact_mode = lax.Precision.HIGHEST
eps_norm = 1e-06

def mm_exact(left_op, right_op):
    return jnp.dot(left_op, right_op, precision=exact_mode, preferred_element_type=jnp.float32)

def layer_norm(values):
    center = values - lax.optimization_barrier(jnp.mean(values, axis=-1, keepdims=True))
    spread = lax.optimization_barrier(jnp.mean(center * center, axis=-1, keepdims=True))
    return center * lax.rsqrt(spread + eps_norm)

def modulate(values, shift_part, scale_part):
    return layer_norm(values) * (1.0 + scale_part) + shift_part

def gelu_tanh(values):
    return 0.5 * values * (1.0 + jnp.tanh(0.7978845608028654 * (values + 0.044715 * values * values * values)))

def tile_layout(lengths, tile_row, tile_col, count_here, tile_count):
    tile_len = (lengths // tile_count).astype(jnp.int32)
    ends_at = jnp.cumsum(tile_len).astype(jnp.int32)
    starts_at = (ends_at - tile_len).astype(jnp.int32)
    place_index = jnp.arange(count_here, dtype=jnp.int32)
    segment = lax.optimization_barrier(jnp.sum((place_index[:, None] >= ends_at[None, :]).astype(jnp.int32), axis=1)).astype(jnp.int32)
    slot_index = jnp.arange(lengths.shape[0], dtype=jnp.int32)
    member = segment[:, None] == slot_index[None, :]
    slot_side = jnp.where(lengths == BIG_LEN, BIG_SIDE, SMALL_SIDE).astype(jnp.int32)
    token_side = lax.optimization_barrier(jnp.sum(jnp.where(member, slot_side[None, :], 0), axis=1)).astype(jnp.int32)
    token_start = lax.optimization_barrier(jnp.sum(jnp.where(member, starts_at[None, :], 0), axis=1)).astype(jnp.int32)
    offset_in = (place_index - token_start).astype(jnp.int32)
    grid_row = tile_row * token_side + offset_in // token_side
    grid_col = tile_col * token_side + offset_in % token_side
    return (segment, member.astype(jnp.float32), grid_row, grid_col)

def sincos_embed(grid_row, grid_col, model_width):
    quarter = model_width // 4
    rates = 1.0 / jnp.power(10000.0, jnp.arange(quarter, dtype=jnp.float32) / quarter)
    row_angle = grid_row.astype(jnp.float32)[:, None] * rates[None, :]
    col_angle = grid_col.astype(jnp.float32)[:, None] * rates[None, :]
    return jnp.concatenate([jnp.sin(row_angle), jnp.cos(row_angle), jnp.sin(col_angle), jnp.cos(col_angle)], axis=1)

def attention(query, keys, values, seg_ids):
    token_total = query.shape[0]
    q_heads = query.reshape(token_total, HEADS, HEAD_DIM)
    k_heads = keys.reshape(token_total, HEADS, HEAD_DIM)
    v_heads = values.reshape(token_total, HEADS, HEAD_DIM)
    scores = low_back(jnp.einsum('qhd,khd->hqk', q_heads, k_heads, precision=exact_mode) * (1.0 / math.sqrt(HEAD_DIM)))
    same_image = (seg_ids[:, None] == seg_ids[None, :])[None, :, :]
    attn_probs = low(jax.nn.softmax(jnp.where(same_image, scores, -1e+30), axis=-1))
    mixed = jnp.einsum('hqk,khd->qhd', attn_probs, v_heads, precision=exact_mode)
    return mixed.reshape(token_total, HEADS * HEAD_DIM)

def block_forward(patch_tok, cond_pack, params, member, position, seg_ids):
    w_patch, b_patch, w_mod, b_mod, w_qkv, b_query, b_value, w_proj, b_proj, w_fc1, b_fc1, w_fc2, b_fc2, w_fmod, b_fmod, w_out, b_out = params
    model_width = w_patch.shape[1]
    act_cond = jax.nn.silu(cond_pack)
    modul = mm_exact(member, mm_exact(act_cond, w_mod) + b_mod)
    final_mod = mm_exact(member, mm_exact(act_cond, w_fmod) + b_fmod)

    def block_of(array, index):
        return array[:, index * model_width:(index + 1) * model_width]
    hidden = mm_exact(patch_tok, w_patch) + b_patch + position
    entry_attn = low(modulate(hidden, block_of(modul, 0), block_of(modul, 1)))
    projected = mm_exact(entry_attn, low(w_qkv))
    query = low(low_back(block_of(projected, 0) + b_query))
    keys = low(low_back(block_of(projected, 1)))
    values = low(low_back(block_of(projected, 2) + b_value))
    attended = low(low_back(attention(query, keys, values, seg_ids)))
    attn_out = low_back(mm_exact(attended, low(w_proj)) + b_proj)
    hidden = hidden + block_of(modul, 2) * attn_out
    entry_mlp = low(modulate(hidden, block_of(modul, 3), block_of(modul, 4)))
    inner_pre = low_back(mm_exact(entry_mlp, low(w_fc1)) + b_fc1)
    activ = low(gelu_tanh(inner_pre))
    mlp_out = low_back(mm_exact(activ, low(w_fc2)) + b_fc2)
    hidden = hidden + block_of(modul, 5) * mlp_out
    entry_out = low(modulate(hidden, block_of(final_mod, 0), block_of(final_mod, 1)))
    return low_back(mm_exact(entry_out, low(w_out)) + b_out)

def reference(patches, cond, image_lengths, cotangent, w_patch, b_patch, w_mod, b_mod, w_qkv, b_query, b_value, w_proj, b_proj, w_fc1, b_fc1, w_fc2, b_fc2, w_fmod, b_fmod, w_out, b_out):
    params = (w_patch, b_patch, w_mod, b_mod, w_qkv, b_query, b_value, w_proj, b_proj, w_fc1, b_fc1, w_fc2, b_fc2, w_fmod, b_fmod, w_out, b_out)
    tile_count = ROWS * COLS
    model_width = w_patch.shape[1]

    def to_packs(array, channels):
        array = array.reshape(GROUPS, tile_count, channels, NPACK, PT)
        array = jnp.transpose(array, (0, 3, 1, 2, 4))
        return array.reshape(GROUPS * NPACK, tile_count, channels, PT)

    def from_packs(array, channels):
        array = array.reshape(GROUPS, NPACK, tile_count, channels, PT)
        array = jnp.transpose(array, (0, 2, 3, 1, 4))
        return array.reshape(GROUPS, ROWS, COLS, channels, NPACK * PT)
    patch_packs = to_packs(patches, PATCH_IN)
    cotan_packs = to_packs(cotangent, OUT_CH)
    cond_packs = cond.reshape(GROUPS * NPACK, IMGS, model_width)
    length_packs = image_lengths.reshape(GROUPS * NPACK, IMGS)

    def one_pack(carry, packed):
        patch_pack, cond_pack, length_pack, cotan_pack = packed
        segments = []
        members = []
        rows_all = []
        cols_all = []
        for tile_index in range(tile_count):
            segment, member, grid_row, grid_col = tile_layout(length_pack, tile_index // COLS, tile_index % COLS, PT, tile_count)
            segments.append(segment)
            members.append(member)
            rows_all.append(grid_row)
            cols_all.append(grid_col)
        seg_ids = jnp.concatenate(segments, axis=0)
        member = jnp.concatenate(members, axis=0)
        position = sincos_embed(jnp.concatenate(rows_all, axis=0), jnp.concatenate(cols_all, axis=0), model_width)
        patch_tok = jnp.transpose(patch_pack, (0, 2, 1)).reshape(tile_count * PT, PATCH_IN)
        cotan_tok = jnp.transpose(cotan_pack, (0, 2, 1)).reshape(tile_count * PT, OUT_CH)

        def forward_fn(patch_in, cond_in, param_in):
            return block_forward(patch_in, cond_in, param_in, member, position, seg_ids)
        result, pullback = jax.vjp(forward_fn, patch_tok, cond_pack, params)
        grad_tok, grad_cnd, grad_prm = pullback(cotan_tok)
        carry = jax.tree.map(lambda acc_val, new_val: acc_val + new_val, carry, grad_prm)
        result_pack = jnp.transpose(result.reshape(tile_count, PT, OUT_CH), (0, 2, 1))
        grad_pack = jnp.transpose(grad_tok.reshape(tile_count, PT, PATCH_IN), (0, 2, 1))
        return (carry, (result_pack, grad_pack, grad_cnd))
    init = tuple((jnp.zeros(p.shape, jnp.float32) for p in params))
    sums, (results, grad_tiles, grad_conds) = lax.scan(one_pack, init, (patch_packs, cond_packs, length_packs, cotan_packs))
    output = from_packs(results, OUT_CH)
    grad_patches = from_packs(grad_tiles, PATCH_IN)
    grad_cond = grad_conds.reshape(GROUPS, NPACK * IMGS, model_width)
    return (output, grad_patches, grad_cond, sums[0], sums[1], sums[2], sums[3], sums[4], sums[5], sums[6], sums[7], sums[8], sums[9], sums[10], sums[11], sums[12], sums[13], sums[14], sums[15], sums[16])
```

```python
import math

import jax
import jax.numpy as jnp
from jax import lax
from jax.sharding import PartitionSpec as P

HEADS = 6
HEAD_DIM = 64
BIG_SIDE = 16
SMALL_SIDE = 8
BIG_LEN = 1024


exact_mode = lax.Precision.HIGHEST
eps_norm = 1e-06


def tile_layout(lengths, tile_row, tile_col, count_here, tile_count):
    tile_len = lengths // tile_count
    ends_at = jnp.cumsum(tile_len)
    starts_at = ends_at - tile_len
    place_index = jnp.arange(count_here, dtype=jnp.int32)
    segment = jnp.sum((place_index[:, None] >= ends_at[None, :]).astype(jnp.int32), axis=1)
    slot_index = jnp.arange(lengths.shape[0], dtype=jnp.int32)
    member = segment[:, None] == slot_index[None, :]
    slot_side = jnp.where(lengths == BIG_LEN, BIG_SIDE, SMALL_SIDE).astype(jnp.int32)
    token_side = jnp.sum(jnp.where(member, slot_side[None, :], 0), axis=1)
    token_start = jnp.sum(jnp.where(member, starts_at[None, :], 0), axis=1)
    offset_in = place_index - token_start
    grid_row = tile_row * token_side + offset_in // token_side
    grid_col = tile_col * token_side + offset_in % token_side
    return (segment, member.astype(jnp.float32), grid_row, grid_col)


def sincos_embed(grid_row, grid_col, model_width):
    quarter = model_width // 4
    rates = 1.0 / jnp.power(10000.0, jnp.arange(quarter, dtype=jnp.float32) / quarter)
    row_angle = grid_row.astype(jnp.float32)[:, None] * rates[None, :]
    col_angle = grid_col.astype(jnp.float32)[:, None] * rates[None, :]
    return jnp.concatenate(
        [jnp.sin(row_angle), jnp.cos(row_angle), jnp.sin(col_angle), jnp.cos(col_angle)], axis=1
    )


def gelu_tanh(values):
    return (
        0.5
        * values
        * (1.0 + jnp.tanh(0.7978845608028654 * (values + 0.044715 * values * values * values)))
    )


def norm_stats(values):
    center = values - jnp.mean(values, axis=1, keepdims=True)
    inv_std = lax.rsqrt(jnp.mean(center * center, axis=1, keepdims=True) + eps_norm)
    return (center * inv_std, inv_std)


def norm_back(grad_in, normed, inv_std):
    return inv_std * (
        grad_in
        - jnp.mean(grad_in, axis=1, keepdims=True)
        - normed * jnp.mean(grad_in * normed, axis=1, keepdims=True)
    )


def contract_rows(left_op, right_op):
    return lax.dot_general(
        left_op, right_op, (((0,), (0,)), ((), ())), preferred_element_type=jnp.float32
    )


def contract_last(left_op, right_op):
    return lax.dot_general(
        left_op, right_op, (((1,), (1,)), ((), ())), preferred_element_type=jnp.float32
    )


def column_block(array, index, model_width):
    return array[:, index * model_width : (index + 1) * model_width]


def heads_of(values):
    return values.reshape(values.shape[0], HEADS, HEAD_DIM)


def bit_swap(array, axis_name, bit):
    size = lax.axis_size(axis_name)
    return lax.ppermute(array, axis_name, [(i, i ^ (1 << bit)) for i in range(size)])


def bit_here(axis_name, bit):
    return (lax.axis_index(axis_name) >> bit) & 1


def join_halves(mine, other, axis_name, bit):
    low_side = bit_here(axis_name, bit) == 0
    return jnp.concatenate(
        [jnp.where(low_side, mine, other), jnp.where(low_side, other, mine)], axis=0
    )


def batch_bits():
    size = lax.axis_size("batch")
    assert size & (size - 1) == 0
    return size.bit_length() - 1


def gather_batch(array):
    for bit in range(batch_bits()):
        array = join_halves(array, bit_swap(array, "batch", bit), "batch", bit)
    return array


def sum_tiles(array):
    array = array + bit_swap(array, "col", 0)
    return array + bit_swap(array, "row", 0)


def sum_everywhere(array):
    array = sum_tiles(array)
    for bit in range(batch_bits()):
        array = array + bit_swap(array, "batch", bit)
    return array


def halve_step(part, axis_name, bit):
    half = part.shape[0] // 2
    here = bit_here(axis_name, bit)
    keep = lax.dynamic_slice_in_dim(part, here * half, half, 0)
    send = lax.dynamic_slice_in_dim(part, (1 - here) * half, half, 0)
    got = bit_swap(send, axis_name, bit)
    return (keep.astype(jnp.float32) + got.astype(jnp.float32)).astype(jnp.bfloat16)


def colour_orders():
    bits = [("batch", bit) for bit in range(batch_bits())]
    first = ("col", 0)
    second = ("row", 0)
    return (
        [first, second] + bits,
        [first] + bits[:2] + [second] + bits[2:],
        [first] + bits[1:2] + [second] + bits[:1] + bits[2:],
    )


def sum_rows(parts):
    orders = colour_orders()
    depth = len(orders[0])
    for step in range(depth):
        parts = [halve_step(part, *order[step]) for part, order in zip(parts, orders)]
    for step in reversed(range(depth)):
        parts = [
            join_halves(part, bit_swap(part, *order[step]), *order[step])
            for part, order in zip(parts, orders)
        ]
    return jnp.concatenate(parts, axis=0)


def slabs(array, width):
    return [array[:, at : at + width] for at in range(0, array.shape[1], width)]


def thirds(slab_list):
    stacked = jnp.concatenate([slab.astype(jnp.bfloat16) for slab in slab_list], axis=0)
    rows = stacked.shape[0] // 3
    return [stacked[at * rows : (at + 1) * rows] for at in range(3)]


def unslab(stacked, first, count, rows):
    return jnp.concatenate(
        [stacked[(first + at) * rows : (first + at + 1) * rows] for at in range(count)], axis=1
    ).astype(jnp.float32)


def body(
    patches,
    cond,
    image_lengths,
    cotangent,
    w_patch,
    b_patch,
    w_mod,
    b_mod,
    w_qkv,
    b_query,
    b_value,
    w_proj,
    b_proj,
    w_fc1,
    b_fc1,
    w_fc2,
    b_fc2,
    w_fmod,
    b_fmod,
    w_out,
    b_out,
):
    model_width = w_patch.shape[1]
    pack_count = image_lengths.shape[1]
    slot_count = image_lengths.shape[2]
    token_count = patches.shape[4]
    tile_tokens = token_count // pack_count
    tile_count = lax.axis_size("row") * lax.axis_size("col")
    tile_row = lax.axis_index("row")
    tile_col = lax.axis_index("col")
    score_scale = 1.0 / math.sqrt(HEAD_DIM)

    def layout_pack(pack_lengths):
        return tile_layout(pack_lengths, tile_row, tile_col, tile_tokens, tile_count)

    segment, member, grid_row, grid_col = jax.vmap(layout_pack)(image_lengths[0])
    segment_all = jnp.tile(segment, (1, tile_count))
    position = sincos_embed(
        grid_row.reshape(token_count), grid_col.reshape(token_count), model_width
    )
    cond_slots = cond[0].reshape(pack_count, slot_count, model_width)
    act_cond = jax.nn.silu(cond_slots)
    mods_img = jnp.einsum("psd,de->pse", act_cond, w_mod, precision=exact_mode) + b_mod
    fmods_img = jnp.einsum("psd,de->pse", act_cond, w_fmod, precision=exact_mode) + b_fmod
    mods_tok = jnp.einsum("pts,pse->pte", member, mods_img, precision=exact_mode).reshape(
        token_count, 6 * model_width
    )
    fmods_tok = jnp.einsum("pts,pse->pte", member, fmods_img, precision=exact_mode).reshape(
        token_count, 2 * model_width
    )

    def score_block(q_heads, k_heads, seg_query, seg_key):
        scores = (
            jnp.einsum("qhd,khd->hqk", q_heads, k_heads, preferred_element_type=jnp.float32)
            * score_scale
        )
        return jnp.where((seg_query[:, None] == seg_key[None, :])[None], scores, -1e30)

    def attend_forward(packed):
        q_pack, k_pack, v_pack, seg_query, seg_key = packed
        scores = score_block(heads_of(q_pack), heads_of(k_pack), seg_query, seg_key)
        row_top = jnp.max(scores, axis=2, keepdims=True)
        exp_scores = jnp.exp(scores - row_top)
        row_total = jnp.sum(exp_scores, axis=2, keepdims=True)
        attn_low = (exp_scores / row_total).astype(jnp.bfloat16)
        mixed = jnp.einsum(
            "hqk,khd->qhd", attn_low, heads_of(v_pack), preferred_element_type=jnp.float32
        )
        return (
            mixed.reshape(q_pack.shape[0], model_width),
            (row_top + jnp.log(row_total))[:, :, 0],
        )

    def query_core(q_pack, k_pack, v_pack, do_pack, log_pack, seg_query, seg_key):
        attn_probs = jnp.exp(
            score_block(heads_of(q_pack), heads_of(k_pack), seg_query, seg_key)
            - log_pack[:, :, None]
        )
        grad_probs = jnp.einsum(
            "qhd,khd->hqk", heads_of(do_pack), heads_of(v_pack), preferred_element_type=jnp.float32
        )
        row_delta = jnp.sum(attn_probs * grad_probs, axis=2)
        grad_scores = (attn_probs * (grad_probs - row_delta[:, :, None])).astype(jnp.bfloat16)
        grad_query = (
            jnp.einsum(
                "hqk,khd->qhd", grad_scores, heads_of(k_pack), preferred_element_type=jnp.float32
            )
            * score_scale
        )
        return (
            grad_query.reshape(q_pack.shape[0], model_width),
            row_delta,
            grad_scores,
            attn_probs,
        )

    def full_side(packed):
        q_pack, k_pack, v_pack, do_pack, log_pack, seg_query, seg_key = packed
        grad_query, row_delta, grad_scores, attn_probs = query_core(
            q_pack, k_pack, v_pack, do_pack, log_pack, seg_query, seg_key
        )
        grad_keys = (
            jnp.einsum(
                "hqk,qhd->khd", grad_scores, heads_of(q_pack), preferred_element_type=jnp.float32
            )
            * score_scale
        )
        grad_values = jnp.einsum(
            "hqk,qhd->khd",
            attn_probs.astype(jnp.bfloat16),
            heads_of(do_pack),
            preferred_element_type=jnp.float32,
        )
        key_total = k_pack.shape[0]
        return (
            grad_query,
            grad_keys.reshape(key_total, model_width),
            grad_values.reshape(key_total, model_width),
        )

    patch_cols = patches[0, 0, 0]
    hidden_in = (
        lax.dot_general(
            patch_cols,
            w_patch,
            (((0,), (0,)), ((), ())),
            precision=exact_mode,
            preferred_element_type=jnp.float32,
        )
        + b_patch
        + position
    )
    normed_one, inv_one = norm_stats(hidden_in)
    scale_one = column_block(mods_tok, 1, model_width)
    entry_one = (normed_one * (1.0 + scale_one) + column_block(mods_tok, 0, model_width)).astype(
        jnp.bfloat16
    )
    w_qkv_low = w_qkv.astype(jnp.bfloat16)
    projected = jnp.dot(entry_one, w_qkv_low, preferred_element_type=jnp.float32)
    query_low = (column_block(projected, 0, model_width) + b_query).astype(jnp.bfloat16)
    keys_low = column_block(projected, 1, model_width).astype(jnp.bfloat16)
    values_low = (column_block(projected, 2, model_width) + b_value).astype(jnp.bfloat16)
    query_tiles = query_low.reshape(pack_count, tile_tokens, model_width)
    key_tiles = keys_low.reshape(pack_count, tile_tokens, model_width)
    value_tiles = values_low.reshape(pack_count, tile_tokens, model_width)
    key_all, value_all = (
        lax.all_gather(key_tiles, ("row", "col"), axis=1, tiled=True),
        lax.all_gather(value_tiles, ("row", "col"), axis=1, tiled=True),
    )
    attended, log_total = lax.map(
        attend_forward, (query_tiles, key_all, value_all, segment, segment_all)
    )
    attended_low = attended.reshape(token_count, model_width).astype(jnp.bfloat16)
    w_proj_low = w_proj.astype(jnp.bfloat16)
    attn_out = jnp.dot(attended_low, w_proj_low, preferred_element_type=jnp.float32) + b_proj
    gate_attn = column_block(mods_tok, 2, model_width)
    hidden_mid = hidden_in + gate_attn * attn_out
    normed_two, inv_two = norm_stats(hidden_mid)
    scale_two = column_block(mods_tok, 4, model_width)
    entry_two = (normed_two * (1.0 + scale_two) + column_block(mods_tok, 3, model_width)).astype(
        jnp.bfloat16
    )
    w_fc1_low = w_fc1.astype(jnp.bfloat16)
    w_fc2_low = w_fc2.astype(jnp.bfloat16)
    inner_pre = jnp.dot(entry_two, w_fc1_low, preferred_element_type=jnp.float32) + b_fc1
    activ_low = gelu_tanh(inner_pre).astype(jnp.bfloat16)
    mlp_out = jnp.dot(activ_low, w_fc2_low, preferred_element_type=jnp.float32) + b_fc2
    gate_mlp = column_block(mods_tok, 5, model_width)
    hidden_out = hidden_mid + gate_mlp * mlp_out
    normed_three, inv_three = norm_stats(hidden_out)
    scale_three = column_block(fmods_tok, 1, model_width)
    entry_three = (
        normed_three * (1.0 + scale_three) + column_block(fmods_tok, 0, model_width)
    ).astype(jnp.bfloat16)
    w_out_low = w_out.astype(jnp.bfloat16)
    result_cols = (
        lax.dot_general(
            w_out_low, entry_three, (((0,), (1,)), ((), ())), preferred_element_type=jnp.float32
        )
        + b_out[:, None]
    )
    grad_out_low = cotangent[0, 0, 0].astype(jnp.bfloat16)
    grad_w_out = lax.dot_general(
        entry_three, grad_out_low, (((0,), (1,)), ((), ())), preferred_element_type=jnp.float32
    )
    grad_b_out = jnp.sum(grad_out_low.astype(jnp.float32), axis=1)
    grad_entry_three = lax.dot_general(
        grad_out_low, w_out_low, (((0,), (1,)), ((), ())), preferred_element_type=jnp.float32
    )
    grad_fmods_tok = jnp.concatenate([grad_entry_three, grad_entry_three * normed_three], axis=1)
    grad_hidden_out = norm_back(grad_entry_three * (1.0 + scale_three), normed_three, inv_three)
    grad_mlp_low = (gate_mlp * grad_hidden_out).astype(jnp.bfloat16)
    grad_gate_mlp = grad_hidden_out * mlp_out
    grad_w_fc2 = contract_rows(activ_low, grad_mlp_low)
    grad_b_fc2 = jnp.sum(grad_mlp_low.astype(jnp.float32), axis=0)
    grad_activ = contract_last(grad_mlp_low, w_fc2_low)
    grad_inner_low = jax.vjp(gelu_tanh, inner_pre)[1](grad_activ)[0].astype(jnp.bfloat16)
    grad_w_fc1 = contract_rows(entry_two, grad_inner_low)
    grad_b_fc1 = jnp.sum(grad_inner_low.astype(jnp.float32), axis=0)
    grad_entry_two = contract_last(grad_inner_low, w_fc1_low)
    grad_hidden_mid = grad_hidden_out + norm_back(
        grad_entry_two * (1.0 + scale_two), normed_two, inv_two
    )
    grad_attn_low = (gate_attn * grad_hidden_mid).astype(jnp.bfloat16)
    grad_gate_attn = grad_hidden_mid * attn_out
    grad_w_proj = contract_rows(attended_low, grad_attn_low)
    grad_b_proj = jnp.sum(grad_attn_low.astype(jnp.float32), axis=0)
    grad_attended_low = contract_last(grad_attn_low, w_proj_low).astype(jnp.bfloat16)
    grad_att_tiles = grad_attended_low.reshape(pack_count, tile_tokens, model_width)
    grad_query, grad_keys_all, grad_values_all = lax.map(
        full_side,
        (query_tiles, key_all, value_all, grad_att_tiles, log_total, segment, segment_all),
    )
    grad_keys, grad_values = (
        lax.psum_scatter(grad_keys_all, ("row", "col"), scatter_dimension=1, tiled=True),
        lax.psum_scatter(grad_values_all, ("row", "col"), scatter_dimension=1, tiled=True),
    )
    grad_query_low = grad_query.reshape(token_count, model_width).astype(jnp.bfloat16)
    grad_keys_low = grad_keys.reshape(token_count, model_width).astype(jnp.bfloat16)
    grad_values_low = grad_values.reshape(token_count, model_width).astype(jnp.bfloat16)
    grad_qkv = jnp.concatenate([grad_query_low, grad_keys_low, grad_values_low], axis=1)
    grad_w_qkv = contract_rows(entry_one, grad_qkv)
    grad_b_query = jnp.sum(grad_query_low.astype(jnp.float32), axis=0)
    grad_b_value = jnp.sum(grad_values_low.astype(jnp.float32), axis=0)
    grad_entry_one = contract_last(grad_qkv, w_qkv_low)
    grad_hidden_in = grad_hidden_mid + norm_back(
        grad_entry_one * (1.0 + scale_one), normed_one, inv_one
    )
    grad_w_patch = lax.dot_general(
        patch_cols,
        grad_hidden_in,
        (((1,), (0,)), ((), ())),
        precision=exact_mode,
        preferred_element_type=jnp.float32,
    )
    grad_b_patch = jnp.sum(grad_hidden_in, axis=0)
    grad_patch_cols = lax.dot_general(
        w_patch,
        grad_hidden_in,
        (((1,), (1,)), ((), ())),
        precision=exact_mode,
        preferred_element_type=jnp.float32,
    )
    grad_mods_tok = jnp.concatenate(
        [
            grad_entry_one,
            grad_entry_one * normed_one,
            grad_gate_attn,
            grad_entry_two,
            grad_entry_two * normed_two,
            grad_gate_mlp,
        ],
        axis=1,
    )
    grad_mods_img = jnp.einsum(
        "pts,pte->pse",
        member,
        grad_mods_tok.reshape(pack_count, tile_tokens, 6 * model_width),
        precision=exact_mode,
    )
    grad_fmods_img = jnp.einsum(
        "pts,pte->pse",
        member,
        grad_fmods_tok.reshape(pack_count, tile_tokens, 2 * model_width),
        precision=exact_mode,
    )
    slot_total = pack_count * slot_count
    grad_slots = jnp.concatenate([grad_mods_img, grad_fmods_img], axis=2).reshape(
        slot_total, 8 * model_width
    )
    grad_slots = sum_tiles(grad_slots)
    grad_slots_all = gather_batch(grad_slots.astype(jnp.bfloat16)).astype(jnp.float32)
    act_all = jax.nn.silu(gather_batch(cond[0]))
    grad_w_mods = lax.dot_general(
        act_all, grad_slots_all, (((0,), (0,)), ((), ())), precision=exact_mode
    )
    grad_b_mods = jnp.sum(grad_slots_all, axis=0)
    grad_act = lax.dot_general(
        grad_slots[:, : 6 * model_width], w_mod, (((1,), (1,)), ((), ())), precision=exact_mode
    ) + lax.dot_general(
        grad_slots[:, 6 * model_width :], w_fmod, (((1,), (1,)), ((), ())), precision=exact_mode
    )
    grad_cond = jax.vjp(jax.nn.silu, cond[0])[1](grad_act)[0][None]
    early = sum_rows(thirds(slabs(grad_w_fc2, model_width) + slabs(grad_w_fc1, model_width)))
    late = sum_rows(thirds(slabs(grad_w_qkv, model_width) + [grad_w_proj]))
    ff_width = w_fc1.shape[1]
    out_width = w_out.shape[1]
    small = jnp.concatenate(
        [
            grad_w_patch,
            grad_w_out.T,
            grad_b_patch[None],
            grad_b_query[None],
            grad_b_value[None],
            grad_b_proj[None],
            grad_b_fc1.reshape(-1, model_width),
            grad_b_fc2[None],
            jnp.pad(grad_b_out, (0, model_width - out_width))[None],
        ],
        axis=0,
    )
    small = sum_everywhere(small)
    patch_rows = w_patch.shape[0]
    at = patch_rows + out_width
    ff_slabs = ff_width // model_width
    summed = (
        small[:patch_rows],
        small[at],
        grad_w_mods[:, : 6 * model_width],
        grad_b_mods[: 6 * model_width],
        unslab(late, 0, 3, model_width),
        small[at + 1],
        small[at + 2],
        unslab(late, 3, 1, model_width),
        small[at + 3],
        unslab(early, ff_slabs, ff_slabs, model_width),
        small[at + 4 : at + 4 + ff_slabs].reshape(ff_width),
        early[:ff_width].astype(jnp.float32),
        small[at + 4 + ff_slabs],
        grad_w_mods[:, 6 * model_width :],
        grad_b_mods[6 * model_width :],
        small[patch_rows:at].T,
        small[at + 5 + ff_slabs, :out_width],
    )
    return (result_cols[None, None, None], grad_patch_cols[None, None, None], grad_cond) + tuple(
        summed
    )


def solution(mesh):
    placed = (
        P("batch", "row", "col", None, None),
        P("batch", None, None),
        P("batch", None, None),
        P("batch", "row", "col", None, None),
        P(),
        P(),
        P(),
        P(),
        P(),
        P(),
        P(),
        P(),
        P(),
        P(),
        P(),
        P(),
        P(),
        P(),
        P(),
        P(),
        P(),
    )
    return jax.shard_map(
        body,
        mesh=mesh,
        in_specs=placed,
        out_specs=(
            P("batch", "row", "col", None, None),
            P("batch", "row", "col", None, None),
            P("batch", None, None),
            P(),
            P(),
            P(),
            P(),
            P(),
            P(),
            P(),
            P(),
            P(),
            P(),
            P(),
            P(),
            P(),
            P(),
            P(),
            P(),
            P(),
        ),
        check_vma=False,
    )
```

```python
import math

import jax
import jax.numpy as jnp
from jax import lax
from jax.experimental import pallas as pl
from jax.experimental.pallas import tpu as pltpu
from jax.sharding import PartitionSpec as P

HEADS = 6
HEAD_DIM = 64
BIG_SIDE = 16
SMALL_SIDE = 8
BIG_LEN = 1024
W = 384
T = 256
ALL = 1024
FF = 1536
PATCH = 16
OUTC = 32
BLOCKS = 4
BLOCK = T // BLOCKS
SMALL_AT = 1536
SLOT_AT = 1600
SLOT_ROWS = 48

exact_mode = lax.Precision.HIGHEST
eps_norm = 1e-06
low = jnp.bfloat16
full = jnp.float32


def mm(left_op, right_op, precision=None):
    return lax.dot_general(
        left_op,
        right_op,
        (((1,), (0,)), ((), ())),
        precision=precision,
        preferred_element_type=full,
    )


def mm_last(left_op, right_op, precision=None):
    return lax.dot_general(
        left_op,
        right_op,
        (((1,), (1,)), ((), ())),
        precision=precision,
        preferred_element_type=full,
    )


def mm_rows(left_op, right_op):
    return lax.dot_general(
        left_op, right_op, (((0,), (0,)), ((), ())), preferred_element_type=full
    )


def norm_stats(values):
    center = values - jnp.mean(values, axis=1, keepdims=True)
    inv_std = lax.rsqrt(jnp.mean(center * center, axis=1, keepdims=True) + eps_norm)
    return (center * inv_std, inv_std)


def norm_back(grad_in, normed, inv_std):
    return inv_std * (
        grad_in
        - jnp.mean(grad_in, axis=1, keepdims=True)
        - normed * jnp.mean(grad_in * normed, axis=1, keepdims=True)
    )


def per_token(mods, index):
    rows = mods[:, index * W : (index + 1) * W]
    return jnp.concatenate(
        [jnp.broadcast_to(rows[b : b + 1], (BLOCK, W)) for b in range(BLOCKS)], axis=0
    )


def block_sums(values):
    return jnp.concatenate(
        [
            jnp.sum(values[b * BLOCK : (b + 1) * BLOCK], axis=0, keepdims=True)
            for b in range(BLOCKS)
        ],
        axis=0,
    )


def same_image(big, rows, cols):
    row_seg = (lax.broadcasted_iota(jnp.int32, (rows, cols), 0) & (T - 1)) >> 6
    col_seg = (lax.broadcasted_iota(jnp.int32, (rows, cols), 1) & (T - 1)) >> 6
    gap = jnp.where(big, 0, row_seg - col_seg)
    return gap == 0


def gelu_parts(u):
    c = 0.7978845608028654
    square = u * u
    t = jnp.tanh(c * (u + 0.044715 * u * square))
    value = 0.5 * u * (1.0 + t)
    slope = 0.5 * (1.0 + t) + 0.5 * u * (1.0 - t * t) * (c * (1.0 + 3.0 * 0.044715 * square))
    return value, slope


def pair_half(rows, half):
    lane = lax.broadcasted_iota(jnp.int32, (rows, 2 * HEAD_DIM), 1)
    return (lane < HEAD_DIM) if half == 0 else (lane >= HEAD_DIM)


def front_kernel(
    meta,
    patches_all,
    cot,
    mods_ref,
    w_embed,
    b_patch,
    b_query,
    b_value,
    b_proj,
    b_fc1,
    b_fc2,
    w_out_t,
    b_out,
    w_qkv_hbm,
    w_proj_hbm,
    w_fc1_hbm,
    w_fc2_hbm,
    result,
    payload,
    qkv_all,
    entry_own,
    normed_own,
    inv_own,
    attended_out,
    grad_attn_out,
    grad_mid_out,
    activ_out,
    grad_mlp_out,
    entry_two_out,
    grad_inner_out,
    small_out,
    slots_out,
    w_qkv_low,
    w_qkv_v,
    w_proj_v,
    w_fc1_v,
    w_fc2_v,
    entry_all,
    mixed_ref,
    stat_ref,
    inner_ref,
    sems,
):
    copies = [
        pltpu.make_async_copy(src, dst, sems.at[at])
        for at, (src, dst) in enumerate(
            (
                (w_qkv_hbm, w_qkv_v),
                (w_proj_hbm, w_proj_v),
                (w_fc1_hbm, w_fc1_v),
                (w_fc2_hbm, w_fc2_v),
            )
        )
    ]
    for copy in copies:
        copy.start()
    big = meta[0] == 1
    tile_row = meta[1]
    tile_col = meta[2]
    token = lax.broadcasted_iota(jnp.int32, (32, ALL), 1)
    tile = token >> 8
    place = token & (T - 1)
    inside = place & 63
    row_here = tile_row ^ (tile & 1)
    col_here = tile_col ^ (tile >> 1)
    grid_row = jnp.where(
        big, row_here * BIG_SIDE + (place >> 4), row_here * SMALL_SIDE + (inside >> 3)
    )
    grid_col = jnp.where(
        big, col_here * BIG_SIDE + (place & 15), col_here * SMALL_SIDE + (inside & 7)
    )
    level = lax.broadcasted_iota(jnp.int32, (32, ALL), 0)
    stacked = jnp.concatenate(
        [
            patches_all[...],
            jnp.where(level == grid_row, 1.0, 0.0),
            jnp.where(level == grid_col, 1.0, 0.0),
        ],
        axis=0,
    )
    hidden_all = mm(stacked.T, w_embed[...], exact_mode) + b_patch[...]
    mods = mods_ref[...]
    shift_a = per_token(mods, 0)
    scale_a = 1.0 + per_token(mods, 1)
    hidden_in = hidden_all[:T]
    for tile_at in range(ALL // T):
        rows = slice(tile_at * T, (tile_at + 1) * T)
        normed, inv_std = norm_stats(hidden_all[rows])
        entry = (normed * scale_a + shift_a).astype(low)
        entry_all[rows] = entry
        if tile_at == 0:
            normed_own[...] = normed
            inv_own[...] = inv_std
            entry_own[...] = entry
    copies[0].wait()
    w_qkv_low[...] = w_qkv_v[...].astype(low)
    entries = entry_all[...]
    qkv_all[:, :W] = (mm(entries, w_qkv_low[:, :W]) + b_query[...]).astype(low)
    qkv_all[:, W : 2 * W] = mm(entries, w_qkv_low[:, W : 2 * W]).astype(low)
    qkv_all[:, 2 * W :] = (mm(entries, w_qkv_low[:, 2 * W :]) + b_value[...]).astype(low)
    allowed = same_image(big, T, ALL)
    lane = lax.broadcasted_iota(jnp.int32, (T, 2 * HEAD_DIM), 1)
    stat = jnp.zeros((T, 2 * HEAD_DIM), full)
    for pair in range(HEADS // 2):
        cols = slice(pair * 2 * HEAD_DIM, (pair + 1) * 2 * HEAD_DIM)
        q_pair = qkv_all[:T, cols] * low(1.0 / math.sqrt(HEAD_DIM))
        k_pair = qkv_all[:, W + cols.start : W + cols.stop]
        v_pair = qkv_all[:, 2 * W + cols.start : 2 * W + cols.stop]
        mixed = []
        for half in range(2):
            q_head = jnp.where(pair_half(T, half), q_pair, low(0.0))
            scores = jnp.where(allowed, mm_last(q_head, k_pair), -1e30)
            row_top = jnp.max(scores, axis=1, keepdims=True)
            exp_scores = jnp.exp(scores - row_top)
            row_total = jnp.sum(exp_scores, axis=1, keepdims=True)
            probs = (exp_scores * (1.0 / row_total)).astype(low)
            mixed.append(mm(probs, v_pair))
            stat = jnp.where(lane == 2 * pair + half, row_top + jnp.log(row_total), stat)
        mixed_ref[:, cols] = jnp.where(pair_half(T, 0), mixed[0], mixed[1])
    attended = mixed_ref[...].astype(low)
    attended_out[...] = attended
    copies[1].wait()
    w_proj_low = w_proj_v[...].astype(low)
    attn_out = mm(attended, w_proj_low) + b_proj[...]
    gate_a = per_token(mods, 2)
    hidden_mid = hidden_in + gate_a * attn_out
    normed_two, inv_two = norm_stats(hidden_mid)
    scale_m = 1.0 + per_token(mods, 4)
    entry_two = (normed_two * scale_m + per_token(mods, 3)).astype(low)
    entry_two_out[...] = entry_two
    copies[2].wait()
    w_fc1_low = w_fc1_v[...].astype(low)
    inner = mm(entry_two, w_fc1_low) + b_fc1[...]
    activ, slope = gelu_parts(inner)
    inner_ref[...] = slope
    activ_low = activ.astype(low)
    activ_out[...] = activ_low
    copies[3].wait()
    w_fc2_low = w_fc2_v[...].astype(low)
    mlp_out = mm(activ_low, w_fc2_low) + b_fc2[...]
    gate_m = per_token(mods, 5)
    hidden_out = hidden_mid + gate_m * mlp_out
    normed_three, inv_three = norm_stats(hidden_out)
    scale_f = 1.0 + per_token(mods, 7)
    entry_three = (normed_three * scale_f + per_token(mods, 6)).astype(low)
    w_out_low = w_out_t[...].astype(low)
    result[...] = mm_last(w_out_low, entry_three) + b_out[...]
    grad_out = cot[...].astype(low)
    small_out[...] = jnp.zeros_like(small_out)
    small_out[PATCH : PATCH + OUTC] = mm(grad_out, entry_three)
    at = PATCH + OUTC
    grad_out_tall = cot[...].T.astype(low)
    grad_b_out = jnp.sum(grad_out_tall.astype(full), axis=0, keepdims=True)
    small_out[at + 9 : at + 10, :OUTC] = grad_b_out
    grad_entry_three = mm(grad_out_tall, w_out_low)
    slots_out[24:28] = block_sums(grad_entry_three)
    slots_out[28:32] = block_sums(grad_entry_three * normed_three)
    grad_hidden_out = norm_back(grad_entry_three * scale_f, normed_three, inv_three)
    grad_mlp = (gate_m * grad_hidden_out).astype(low)
    grad_mlp_out[...] = grad_mlp
    slots_out[20:24] = block_sums(grad_hidden_out * mlp_out)
    small_out[at + 8 : at + 9] = jnp.sum(grad_mlp.astype(full), axis=0, keepdims=True)
    grad_activ = mm_last(grad_mlp, w_fc2_low)
    grad_inner = (grad_activ * inner_ref[...]).astype(low)
    grad_inner_out[...] = grad_inner
    grad_b_fc1 = jnp.sum(grad_inner.astype(full), axis=0, keepdims=True)
    for slab in range(FF // W):
        small_out[at + 4 + slab : at + 5 + slab] = grad_b_fc1[:, slab * W : (slab + 1) * W]
    grad_entry_two = mm_last(grad_inner, w_fc1_low)
    slots_out[12:16] = block_sums(grad_entry_two)
    slots_out[16:20] = block_sums(grad_entry_two * normed_two)
    grad_hidden_mid = grad_hidden_out + norm_back(grad_entry_two * scale_m, normed_two, inv_two)
    grad_mid_out[...] = grad_hidden_mid
    grad_attn = (gate_a * grad_hidden_mid).astype(low)
    grad_attn_out[...] = grad_attn
    slots_out[0:8] = jnp.zeros((8, W), full)
    slots_out[8:12] = block_sums(grad_hidden_mid * attn_out)
    small_out[at + 3 : at + 4] = jnp.sum(grad_attn.astype(full), axis=0, keepdims=True)
    grad_attended = mm_last(grad_attn, w_proj_low).astype(low)
    payload[:, :W] = grad_attended
    for pair in range(HEADS // 2):
        cols = slice(pair * 2 * HEAD_DIM, (pair + 1) * 2 * HEAD_DIM)
        product = grad_attended[:, cols].astype(full) * mixed_ref[:, cols]
        for half in range(2):
            picked = jnp.where(pair_half(T, half), product, 0.0)
            stat = jnp.where(
                lane == 8 + 2 * pair + half, jnp.sum(picked, axis=1, keepdims=True), stat
            )
    stat_ref[...] = stat
    first = stat.astype(low).astype(full)
    rest = stat - first
    second = rest.astype(low).astype(full)
    third = rest - second
    payload[:, W:] = (first + pltpu.roll(second, 16, 1) + pltpu.roll(third, 32, 1)).astype(low)


def query_kernel(
    meta,
    qkv_all,
    payload,
    stat_ref,
    activ,
    grad_mlp,
    entry_two,
    grad_inner,
    grad_query_out,
    grad_fc2,
    grad_fc1,
):
    big = meta[0] == 1
    allowed = same_image(big, T, ALL)
    for pair in range(HEADS // 2):
        cols = slice(pair * 2 * HEAD_DIM, (pair + 1) * 2 * HEAD_DIM)
        q_pair = qkv_all[:T, cols] * low(1.0 / math.sqrt(HEAD_DIM))
        k_pair = qkv_all[:, W + cols.start : W + cols.stop]
        v_pair = qkv_all[:, 2 * W + cols.start : 2 * W + cols.stop]
        do_pair = payload[:, cols]
        grads = []
        for half in range(2):
            head = 2 * pair + half
            q_head = jnp.where(pair_half(T, half), q_pair, low(0.0))
            do_head = jnp.where(pair_half(T, half), do_pair, low(0.0))
            scores = jnp.where(allowed, mm_last(q_head, k_pair), -1e30)
            probs = jnp.exp(scores - stat_ref[:, head : head + 1])
            grad_probs = mm_last(do_head, v_pair)
            grad_scores = (probs * (grad_probs - stat_ref[:, 8 + head : 9 + head])).astype(low)
            grads.append(mm(grad_scores, k_pair))
        grad_query_out[:, cols] = (
            jnp.where(pair_half(T, 0), grads[0], grads[1]) * (1.0 / math.sqrt(HEAD_DIM))
        ).astype(low)
    grad_fc2[...] = mm_rows(activ[...], grad_mlp[...]).astype(low)
    entry = entry_two[...]
    for slab in range(FF // W):
        grad_fc1[slab * W : (slab + 1) * W] = mm_rows(
            entry, grad_inner[:, slab * W : (slab + 1) * W]
        ).astype(low)


def key_kernel(
    meta,
    qkv_all,
    payload_all,
    grad_query,
    entry_own,
    normed_own,
    inv_own,
    attended,
    grad_attn,
    grad_mid,
    small,
    slots,
    mods_ref,
    act_ref,
    patches,
    w_patch,
    w_qkv_low,
    bundle,
    grad_patches,
    gk_ref,
    gv_ref,
):
    big = meta[0] == 1
    allowed = same_image(big, T, ALL)
    packed = payload_all[:, W:].astype(full)
    stat = packed + pltpu.roll(packed, 112, 1) + pltpu.roll(packed, 96, 1)
    stat_t = stat.T
    for pair in range(HEADS // 2):
        cols = slice(pair * 2 * HEAD_DIM, (pair + 1) * 2 * HEAD_DIM)
        q_pair = qkv_all[:, cols]
        k_pair = qkv_all[:T, W + cols.start : W + cols.stop] * low(1.0 / math.sqrt(HEAD_DIM))
        v_pair = qkv_all[:T, 2 * W + cols.start : 2 * W + cols.stop]
        do_pair = payload_all[:, cols]
        grad_k = []
        grad_v = []
        for half in range(2):
            head = 2 * pair + half
            k_head = jnp.where(pair_half(T, half), k_pair, low(0.0))
            v_head = jnp.where(pair_half(T, half), v_pair, low(0.0))
            scores = jnp.where(allowed, mm_last(k_head, q_pair), -1e30)
            probs = jnp.exp(scores - stat_t[head : head + 1])
            grad_probs = mm_last(v_head, do_pair)
            grad_scores = (probs * (grad_probs - stat_t[8 + head : 9 + head])).astype(low)
            grad_v.append(mm(probs.astype(low), do_pair))
            grad_k.append(mm(grad_scores, q_pair))
        gk_ref[:, cols] = (
            jnp.where(pair_half(T, 0), grad_k[0], grad_k[1]) * (1.0 / math.sqrt(HEAD_DIM))
        ).astype(low)
        gv_ref[:, cols] = jnp.where(pair_half(T, 0), grad_v[0], grad_v[1]).astype(low)
    entry = entry_own[...]
    grad_q = grad_query[...]
    grad_k = gk_ref[...]
    grad_v = gv_ref[...]
    bundle[:W] = mm_rows(entry, grad_q).astype(low)
    bundle[W : 2 * W] = mm_rows(entry, grad_k).astype(low)
    bundle[2 * W : 3 * W] = mm_rows(entry, grad_v).astype(low)
    bundle[3 * W : 4 * W] = mm_rows(attended[...], grad_attn[...]).astype(low)
    grad_entry = (
        mm_last(grad_q, w_qkv_low[:, :W])
        + mm_last(grad_k, w_qkv_low[:, W : 2 * W])
        + mm_last(grad_v, w_qkv_low[:, 2 * W :])
    )
    normed = normed_own[...]
    scale_a = 1.0 + per_token(mods_ref[...], 1)
    grad_in = grad_mid[...] + norm_back(grad_entry * scale_a, normed, inv_own[...])
    grad_patches[...] = mm_last(w_patch[...], grad_in, exact_mode)
    at = PATCH + OUTC
    line = lax.broadcasted_iota(jnp.int32, small.shape, 0)
    tail = small[...]
    tail = jnp.where(line == at, jnp.sum(grad_in, axis=0, keepdims=True), tail)
    tail = jnp.where(line == at + 1, jnp.sum(grad_q.astype(full), axis=0, keepdims=True), tail)
    tail = jnp.where(line == at + 2, jnp.sum(grad_v.astype(full), axis=0, keepdims=True), tail)
    grad_w_patch = mm(patches[...], grad_in, exact_mode)
    tail = jnp.concatenate([grad_w_patch, tail[PATCH:]], axis=0)
    bundle[SMALL_AT:SLOT_AT] = tail.astype(low)
    bundle[SLOT_AT:] = jnp.zeros((bundle.shape[0] - SLOT_AT, W), low)
    late = jnp.concatenate([block_sums(grad_entry), block_sums(grad_entry * normed)], axis=0)
    sums = jnp.concatenate([late, slots[8:]], axis=0)
    joined = []
    slot_line = lax.broadcasted_iota(jnp.int32, (BLOCKS, W), 0)
    for block in range(8):
        part = sums[4 * block : 4 * block + 4]
        whole = jnp.where(slot_line == 0, jnp.sum(part, axis=0, keepdims=True), 0.0)
        joined.append(jnp.where(big, whole, part))
    first_tile = (meta[1] == 0) & (meta[2] == 0)
    joined.append(jnp.where(first_tile, act_ref[...], 0.0))
    joined.append(jnp.zeros((SLOT_ROWS - 36, W), full))
    start = pl.multiple_of(SLOT_AT + meta[3] * SLOT_ROWS, 16)
    bundle[pl.ds(start, SLOT_ROWS)] = jnp.concatenate(joined, axis=0).astype(low)


def bit_swap(array, axis_name, bit):
    size = lax.axis_size(axis_name)
    return lax.ppermute(array, axis_name, [(i, i ^ (1 << bit)) for i in range(size)])


def bit_here(axis_name, bit):
    return (lax.axis_index(axis_name) >> bit) & 1


def join_halves(mine, other, axis_name, bit):
    low_side = bit_here(axis_name, bit) == 0
    return jnp.concatenate(
        [jnp.where(low_side, mine, other), jnp.where(low_side, other, mine)], axis=0
    )


def batch_bits():
    size = lax.axis_size("batch")
    assert size & (size - 1) == 0
    return size.bit_length() - 1


def halve_step(part, axis_name, bit):
    half = part.shape[0] // 2
    here = bit_here(axis_name, bit)
    keep = lax.dynamic_slice_in_dim(part, here * half, half, 0)
    send = lax.dynamic_slice_in_dim(part, (1 - here) * half, half, 0)
    got = bit_swap(send, axis_name, bit)
    return (keep.astype(jnp.float32) + got.astype(jnp.float32)).astype(jnp.bfloat16)


def colour_orders():
    bits = [("batch", bit) for bit in range(batch_bits())]
    first = ("col", 0)
    second = ("row", 0)
    return (
        [first, second] + bits,
        [first] + bits[:2] + [second] + bits[2:],
        [first] + bits[1:2] + [second] + bits[:1] + bits[2:],
    )


def sum_rows(parts):
    orders = colour_orders()
    depth = len(orders[0])
    for step in range(depth):
        parts = [halve_step(part, *order[step]) for part, order in zip(parts, orders)]
    for step in reversed(range(depth)):
        parts = [
            join_halves(part, bit_swap(part, *order[step]), *order[step])
            for part, order in zip(parts, orders)
        ]
    return parts


def shaped(*pairs):
    return [jax.ShapeDtypeStruct(shape, kind) for shape, kind in pairs]


vmem = pl.BlockSpec(memory_space=pltpu.VMEM)
smem = pl.BlockSpec(memory_space=pltpu.SMEM)
hbm = pl.BlockSpec(memory_space=pl.ANY)


def unslab(stacked, first, count):
    return jnp.concatenate(
        [stacked[(first + at) * W : (first + at + 1) * W] for at in range(count)], axis=1
    ).astype(full)


def position_table():
    quarter = W // 4
    rates = 1.0 / jnp.power(10000.0, jnp.arange(quarter, dtype=full) / quarter)
    angle = jnp.arange(32, dtype=full)[:, None] * rates[None, :]
    return jnp.concatenate([jnp.sin(angle), jnp.cos(angle)], axis=1)


def gather_tiles(array, axis):
    array = jnp.concatenate([array, bit_swap(array, "row", 0)], axis=axis)
    return jnp.concatenate([array, bit_swap(array, "col", 0)], axis=axis)


def body(
    patches,
    cond,
    image_lengths,
    cotangent,
    w_patch,
    b_patch,
    w_mod,
    b_mod,
    w_qkv,
    b_query,
    b_value,
    w_proj,
    b_proj,
    w_fc1,
    b_fc1,
    w_fc2,
    b_fc2,
    w_fmod,
    b_fmod,
    w_out,
    b_out,
):
    groups = lax.axis_size("batch")
    devices = groups * lax.axis_size("row") * lax.axis_size("col")
    slot_count = image_lengths.shape[2]
    patch_cols = patches[0, 0, 0]
    patches_all = gather_tiles(patch_cols, 1)
    big = image_lengths[0, 0, 0] == BIG_LEN
    group = lax.axis_index("batch")
    meta = jnp.stack(
        [big.astype(jnp.int32), lax.axis_index("row"), lax.axis_index("col"), group]
    ).astype(jnp.int32)
    act = jax.nn.silu(cond[0])
    mods = jnp.concatenate(
        [
            jnp.dot(act, w_mod, precision=exact_mode) + b_mod,
            jnp.dot(act, w_fmod, precision=exact_mode) + b_fmod,
        ],
        axis=1,
    )
    mods = jnp.where(big, mods[:1], mods)
    table = position_table()
    blank = jnp.zeros_like(table)
    w_embed = jnp.concatenate(
        [
            w_patch,
            jnp.concatenate([table, blank], axis=1),
            jnp.concatenate([blank, table], axis=1),
        ],
        axis=0,
    )
    (
        result,
        payload,
        qkv_all,
        entry_own,
        normed_own,
        inv_own,
        attended,
        grad_attn,
        grad_mid,
        activ,
        grad_mlp,
        entry_two,
        grad_inner,
        small,
        slots,
        w_qkv_low,
        stat,
    ) = pl.pallas_call(
        lambda *refs: front_kernel(
            *refs[:33], *refs[34:40], refs[33], *refs[40:]
        ),
        name="front",
        in_specs=[smem] + [vmem] * 12 + [hbm] * 4,
        out_specs=[vmem] * 17,
        out_shape=shaped(
            ((OUTC, T), full),
            ((T, W + 128), low),
            ((ALL, 3 * W), low),
            ((T, W), low),
            ((T, W), full),
            ((T, 1), full),
            ((T, W), low),
            ((T, W), low),
            ((T, W), full),
            ((T, FF), low),
            ((T, W), low),
            ((T, W), low),
            ((T, FF), low),
            ((64, W), full),
            ((32, W), full),
            ((W, 3 * W), low),
            ((T, 128), full),
        ),
        scratch_shapes=[
            pltpu.VMEM((W, 3 * W), full),
            pltpu.VMEM((W, W), full),
            pltpu.VMEM((W, FF), full),
            pltpu.VMEM((FF, W), full),
            pltpu.VMEM((ALL, W), low),
            pltpu.VMEM((T, W), full),
            pltpu.VMEM((T, FF), full),
            pltpu.SemaphoreType.DMA((4,)),
        ],
    )(
        meta,
        patches_all,
        cotangent[0, 0, 0],
        mods,
        w_embed,
        b_patch[None],
        b_query[None],
        b_value[None],
        b_proj[None],
        b_fc1[None],
        b_fc2[None],
        w_out.T,
        b_out[:, None],
        w_qkv,
        w_proj,
        w_fc1,
        w_fc2,
    )
    payload_all = gather_tiles(payload, 0)
    grad_query, grad_fc2, grad_fc1 = pl.pallas_call(
        query_kernel,
        name="query_side",
        in_specs=[smem] + [vmem] * 7,
        out_specs=[vmem] * 3,
        out_shape=shaped(((T, W), low), ((FF, W), low), ((FF, W), low)),
    )(meta, qkv_all, payload, stat, activ, grad_mlp, entry_two, grad_inner)
    unit = 16 * devices
    rows = -(-(SLOT_AT + groups * SLOT_ROWS) // unit) * unit
    bundle, grad_patch_cols = pl.pallas_call(
        key_kernel,
        name="key_side",
        in_specs=[smem] + [vmem] * 16,
        out_specs=[vmem] * 2,
        out_shape=shaped(((rows, W), low), ((PATCH, T), full)),
        scratch_shapes=[pltpu.VMEM((T, W), low), pltpu.VMEM((T, W), low)],
    )(
        meta,
        qkv_all,
        payload_all,
        grad_query,
        entry_own,
        normed_own,
        inv_own,
        attended,
        grad_attn,
        grad_mid,
        small,
        slots,
        mods,
        act,
        patch_cols,
        w_patch,
        w_qkv_low,
    )
    late, fc1_sum, fc2_sum = sum_rows([bundle, grad_fc1, grad_fc2])
    tail = late[SMALL_AT:SLOT_AT].astype(full)
    by_group = late[SLOT_AT : SLOT_AT + groups * SLOT_ROWS].reshape(groups, SLOT_ROWS, W)
    grad_slots_all = jnp.concatenate(
        [
            by_group[:, 4 * block : 4 * block + 4].reshape(groups * slot_count, W)
            for block in range(8)
        ],
        axis=1,
    )
    act_all = by_group[:, 32:36].reshape(groups * slot_count, W)
    grad_w_mods = lax.dot_general(
        act_all, grad_slots_all, (((0,), (0,)), ((), ())), preferred_element_type=full
    )
    grad_b_mods = jnp.sum(grad_slots_all.astype(full), axis=0)
    grad_slots = lax.dynamic_slice_in_dim(grad_slots_all, group * slot_count, slot_count, 0).astype(
        full
    )
    grad_act = lax.dot_general(
        grad_slots[:, : 6 * W], w_mod, (((1,), (1,)), ((), ())), precision=exact_mode
    ) + lax.dot_general(
        grad_slots[:, 6 * W :], w_fmod, (((1,), (1,)), ((), ())), precision=exact_mode
    )
    grad_cond = jax.vjp(jax.nn.silu, cond[0])[1](grad_act)[0][None]
    at = PATCH + OUTC
    summed = (
        tail[:PATCH],
        tail[at],
        grad_w_mods[:, : 6 * W],
        grad_b_mods[: 6 * W],
        unslab(late, 0, 3),
        tail[at + 1],
        tail[at + 2],
        unslab(late, 3, 1),
        tail[at + 3],
        unslab(fc1_sum, 0, FF // W),
        tail[at + 4 : at + 8].reshape(FF),
        fc2_sum.astype(full),
        tail[at + 8],
        grad_w_mods[:, 6 * W :],
        grad_b_mods[6 * W :],
        tail[PATCH:at].T,
        tail[at + 9, :OUTC],
    )
    return (result[None, None, None], grad_patch_cols[None, None, None], grad_cond) + tuple(
        summed
    )


def solution(mesh):
    placed = (
        P("batch", "row", "col", None, None),
        P("batch", None, None),
        P("batch", None, None),
        P("batch", "row", "col", None, None),
        P(),
        P(),
        P(),
        P(),
        P(),
        P(),
        P(),
        P(),
        P(),
        P(),
        P(),
        P(),
        P(),
        P(),
        P(),
        P(),
        P(),
    )
    return jax.shard_map(
        body,
        mesh=mesh,
        in_specs=placed,
        out_specs=(
            P("batch", "row", "col", None, None),
            P("batch", "row", "col", None, None),
            P("batch", None, None),
            P(),
            P(),
            P(),
            P(),
            P(),
            P(),
            P(),
            P(),
            P(),
            P(),
            P(),
            P(),
            P(),
            P(),
            P(),
            P(),
            P(),
        ),
        check_vma=False,
    )
```

```python
import math

import jax
import jax.numpy as jnp
from jax import lax
from jax.experimental import pallas as pl
from jax.experimental.pallas import tpu as pltpu
from jax.sharding import PartitionSpec as P

HEADS = 6
HEAD_DIM = 64
BIG_SIDE = 16
SMALL_SIDE = 8
BIG_LEN = 1024
W = 384
T = 256
ALL = 1024
FF = 1536
PATCH = 16
OUTC = 32
BLOCKS = 4
BLOCK = T // BLOCKS
EARLY_SMALL = 1536
EARLY_SLOTS = 1584
EARLY_STEP = 32
LATE_SMALL = 384
LATE_SLOTS = 416
LATE_STEP = 16

exact_mode = lax.Precision.HIGHEST
eps_norm = 1e-06
low = jnp.bfloat16
full = jnp.float32


def mm(left_op, right_op, precision=None):
    return lax.dot_general(
        left_op,
        right_op,
        (((1,), (0,)), ((), ())),
        precision=precision,
        preferred_element_type=full,
    )


def mm_last(left_op, right_op, precision=None):
    return lax.dot_general(
        left_op,
        right_op,
        (((1,), (1,)), ((), ())),
        precision=precision,
        preferred_element_type=full,
    )


def mm_rows(left_op, right_op):
    return lax.dot_general(
        left_op, right_op, (((0,), (0,)), ((), ())), preferred_element_type=full
    )


def norm_stats(values):
    center = values - jnp.mean(values, axis=1, keepdims=True)
    inv_std = lax.rsqrt(jnp.mean(center * center, axis=1, keepdims=True) + eps_norm)
    return (center * inv_std, inv_std)


def norm_back(grad_in, normed, inv_std):
    return inv_std * (
        grad_in
        - jnp.mean(grad_in, axis=1, keepdims=True)
        - normed * jnp.mean(grad_in * normed, axis=1, keepdims=True)
    )


def row_of(ref):
    return ref[...].reshape(1, ref.shape[0])


def per_token(mods, index):
    rows = mods[:, index * W : (index + 1) * W]
    return jnp.concatenate(
        [jnp.broadcast_to(rows[b : b + 1], (BLOCK, W)) for b in range(BLOCKS)], axis=0
    )


def block_sums(values):
    return jnp.concatenate(
        [
            jnp.sum(values[b * BLOCK : (b + 1) * BLOCK], axis=0, keepdims=True)
            for b in range(BLOCKS)
        ],
        axis=0,
    )


def same_image(big, rows, cols):
    row_seg = (lax.broadcasted_iota(jnp.int32, (rows, cols), 0) & (T - 1)) >> 6
    col_seg = (lax.broadcasted_iota(jnp.int32, (rows, cols), 1) & (T - 1)) >> 6
    gap = jnp.where(big, 0, row_seg - col_seg)
    return gap == 0


def gelu_parts(u):
    c = 0.7978845608028654
    square = u * u
    t = jnp.tanh(c * (u + 0.044715 * u * square))
    value = 0.5 * u * (1.0 + t)
    slope = 0.5 * (1.0 + t) + 0.5 * u * (1.0 - t * t) * (c * (1.0 + 3.0 * 0.044715 * square))
    return value, slope


def pair_half(rows, half):
    lane = lax.broadcasted_iota(jnp.int32, (rows, 2 * HEAD_DIM), 1)
    return (lane < HEAD_DIM) if half == 0 else (lane >= HEAD_DIM)


def front_kernel(
    meta,
    patch_own,
    patch_row,
    patch_col,
    patch_both,
    cot,
    mods_ref,
    w_patch,
    table,
    b_patch,
    b_query,
    b_value,
    b_proj,
    b_fc1,
    b_fc2,
    w_out,
    b_out,
    w_qkv_hbm,
    w_proj_hbm,
    w_fc1_hbm,
    w_fc2_hbm,
    result,
    payload,
    qkv_all,
    entry_own,
    normed_own,
    inv_own,
    attended_out,
    grad_attn_out,
    grad_mid_out,
    activ_out,
    grad_mlp_out,
    entry_two_out,
    grad_inner_out,
    small_out,
    slots_out,
    w_qkv_low,
    w_qkv_v,
    w_proj_v,
    w_fc1_v,
    w_fc2_v,
    entry_all,
    mixed_ref,
    stat_ref,
    inner_ref,
    sems,
):
    copies = [
        pltpu.make_async_copy(src, dst, sems.at[at])
        for at, (src, dst) in enumerate(
            (
                (w_qkv_hbm, w_qkv_v),
                (w_proj_hbm, w_proj_v),
                (w_fc1_hbm, w_fc1_v),
                (w_fc2_hbm, w_fc2_v),
            )
        )
    ]
    for copy in copies:
        copy.start()
    big = meta[0] == 1
    tile_row = meta[1]
    tile_col = meta[2]
    token = lax.broadcasted_iota(jnp.int32, (32, ALL), 1)
    tile = token >> 8
    place = token & (T - 1)
    inside = place & 63
    row_here = tile_row ^ (tile & 1)
    col_here = tile_col ^ (tile >> 1)
    grid_row = jnp.where(
        big, row_here * BIG_SIDE + (place >> 4), row_here * SMALL_SIDE + (inside >> 3)
    )
    grid_col = jnp.where(
        big, col_here * BIG_SIDE + (place & 15), col_here * SMALL_SIDE + (inside & 7)
    )
    level = lax.broadcasted_iota(jnp.int32, (32, ALL), 0)
    stacked = jnp.concatenate(
        [
            jnp.concatenate(
                [patch_own[...], patch_row[...], patch_col[...], patch_both[...]], axis=1
            ),
            jnp.where(level == grid_row, 1.0, 0.0),
            jnp.where(level == grid_col, 1.0, 0.0),
        ],
        axis=0,
    )
    w_embed = jnp.concatenate([w_patch[...], table[...]], axis=0)
    hidden_all = mm(stacked.T, w_embed, exact_mode) + row_of(b_patch)
    mods = mods_ref[...]
    shift_a = per_token(mods, 0)
    scale_a = 1.0 + per_token(mods, 1)
    hidden_in = hidden_all[:T]
    for tile_at in range(ALL // T):
        rows = slice(tile_at * T, (tile_at + 1) * T)
        normed, inv_std = norm_stats(hidden_all[rows])
        entry = (normed * scale_a + shift_a).astype(low)
        entry_all[rows] = entry
        if tile_at == 0:
            normed_own[...] = normed
            inv_own[...] = inv_std
            entry_own[...] = entry
    copies[0].wait()
    w_qkv_low[...] = w_qkv_v[...].astype(low)
    entries = entry_all[...]
    qkv_all[:, :W] = (mm(entries, w_qkv_low[:, :W]) + row_of(b_query)).astype(low)
    qkv_all[:, W : 2 * W] = mm(entries, w_qkv_low[:, W : 2 * W]).astype(low)
    qkv_all[:, 2 * W :] = (mm(entries, w_qkv_low[:, 2 * W :]) + row_of(b_value)).astype(low)
    allowed = same_image(big, T, ALL)
    lane = lax.broadcasted_iota(jnp.int32, (T, 2 * HEAD_DIM), 1)
    stat = jnp.zeros((T, 2 * HEAD_DIM), full)
    for pair in range(HEADS // 2):
        cols = slice(pair * 2 * HEAD_DIM, (pair + 1) * 2 * HEAD_DIM)
        q_pair = qkv_all[:T, cols] * low(1.0 / math.sqrt(HEAD_DIM))
        k_pair = qkv_all[:, W + cols.start : W + cols.stop]
        v_pair = qkv_all[:, 2 * W + cols.start : 2 * W + cols.stop]
        mixed = []
        for half in range(2):
            q_head = jnp.where(pair_half(T, half), q_pair, low(0.0))
            scores = jnp.where(allowed, mm_last(q_head, k_pair), -1e30)
            row_top = jnp.max(scores, axis=1, keepdims=True)
            exp_scores = jnp.exp(scores - row_top)
            row_total = jnp.sum(exp_scores, axis=1, keepdims=True)
            probs = (exp_scores * (1.0 / row_total)).astype(low)
            mixed.append(mm(probs, v_pair))
            stat = jnp.where(lane == 2 * pair + half, row_top + jnp.log(row_total), stat)
        mixed_ref[:, cols] = jnp.where(pair_half(T, 0), mixed[0], mixed[1])
    attended = mixed_ref[...].astype(low)
    attended_out[...] = attended
    copies[1].wait()
    w_proj_low = w_proj_v[...].astype(low)
    attn_out = mm(attended, w_proj_low) + row_of(b_proj)
    gate_a = per_token(mods, 2)
    hidden_mid = hidden_in + gate_a * attn_out
    normed_two, inv_two = norm_stats(hidden_mid)
    scale_m = 1.0 + per_token(mods, 4)
    entry_two = (normed_two * scale_m + per_token(mods, 3)).astype(low)
    entry_two_out[...] = entry_two
    copies[2].wait()
    w_fc1_low = w_fc1_v[...].astype(low)
    inner = mm(entry_two, w_fc1_low) + row_of(b_fc1)
    activ, slope = gelu_parts(inner)
    inner_ref[...] = slope
    activ_low = activ.astype(low)
    activ_out[...] = activ_low
    copies[3].wait()
    w_fc2_low = w_fc2_v[...].astype(low)
    mlp_out = mm(activ_low, w_fc2_low) + row_of(b_fc2)
    gate_m = per_token(mods, 5)
    hidden_out = hidden_mid + gate_m * mlp_out
    normed_three, inv_three = norm_stats(hidden_out)
    scale_f = 1.0 + per_token(mods, 7)
    entry_three = (normed_three * scale_f + per_token(mods, 6)).astype(low)
    w_out_low = w_out[...].T.astype(low)
    out_bias = jnp.broadcast_to(row_of(b_out), (8, OUTC)).T[:, :1]
    result[...] = mm_last(w_out_low, entry_three) + out_bias
    grad_out = cot[...].astype(low)
    small_out[...] = jnp.zeros_like(small_out)
    small_out[:OUTC] = mm(grad_out, entry_three)
    at = OUTC
    grad_out_tall = cot[...].T.astype(low)
    grad_b_out = jnp.sum(grad_out_tall.astype(full), axis=0, keepdims=True)
    small_out[at + 6 : at + 7, :OUTC] = grad_b_out
    grad_entry_three = mm(grad_out_tall, w_out_low)
    slots_out[16:20] = block_sums(grad_entry_three)
    slots_out[20:24] = block_sums(grad_entry_three * normed_three)
    grad_hidden_out = norm_back(grad_entry_three * scale_f, normed_three, inv_three)
    grad_mlp = (gate_m * grad_hidden_out).astype(low)
    grad_mlp_out[...] = grad_mlp
    slots_out[12:16] = block_sums(grad_hidden_out * mlp_out)
    small_out[at + 5 : at + 6] = jnp.sum(grad_mlp.astype(full), axis=0, keepdims=True)
    grad_activ = mm_last(grad_mlp, w_fc2_low)
    grad_inner = (grad_activ * inner_ref[...]).astype(low)
    grad_inner_out[...] = grad_inner
    grad_b_fc1 = jnp.sum(grad_inner.astype(full), axis=0, keepdims=True)
    for slab in range(FF // W):
        small_out[at + 1 + slab : at + 2 + slab] = grad_b_fc1[:, slab * W : (slab + 1) * W]
    grad_entry_two = mm_last(grad_inner, w_fc1_low)
    slots_out[4:8] = block_sums(grad_entry_two)
    slots_out[8:12] = block_sums(grad_entry_two * normed_two)
    grad_hidden_mid = grad_hidden_out + norm_back(grad_entry_two * scale_m, normed_two, inv_two)
    grad_mid_out[...] = grad_hidden_mid
    grad_attn = (gate_a * grad_hidden_mid).astype(low)
    grad_attn_out[...] = grad_attn
    slots_out[0:4] = block_sums(grad_hidden_mid * attn_out)
    small_out[at : at + 1] = jnp.sum(grad_attn.astype(full), axis=0, keepdims=True)
    grad_attended = mm_last(grad_attn, w_proj_low).astype(low)
    payload[:, :W] = grad_attended
    for pair in range(HEADS // 2):
        cols = slice(pair * 2 * HEAD_DIM, (pair + 1) * 2 * HEAD_DIM)
        product = grad_attended[:, cols].astype(full) * mixed_ref[:, cols]
        for half in range(2):
            picked = jnp.where(pair_half(T, half), product, 0.0)
            stat = jnp.where(
                lane == 8 + 2 * pair + half, jnp.sum(picked, axis=1, keepdims=True), stat
            )
    stat_ref[...] = stat
    first = stat.astype(low).astype(full)
    rest = stat - first
    second = rest.astype(low).astype(full)
    third = rest - second
    payload[:, W:] = (first + pltpu.roll(second, 16, 1) + pltpu.roll(third, 32, 1)).astype(low)


def query_kernel(
    meta,
    qkv_all,
    payload,
    stat_ref,
    grad_query_out,
):
    big = meta[0] == 1
    allowed = same_image(big, T, ALL)
    for pair in range(HEADS // 2):
        cols = slice(pair * 2 * HEAD_DIM, (pair + 1) * 2 * HEAD_DIM)
        q_pair = qkv_all[:T, cols] * low(1.0 / math.sqrt(HEAD_DIM))
        k_pair = qkv_all[:, W + cols.start : W + cols.stop]
        v_pair = qkv_all[:, 2 * W + cols.start : 2 * W + cols.stop]
        do_pair = payload[:, cols]
        grads = []
        for half in range(2):
            head = 2 * pair + half
            q_head = jnp.where(pair_half(T, half), q_pair, low(0.0))
            do_head = jnp.where(pair_half(T, half), do_pair, low(0.0))
            scores = jnp.where(allowed, mm_last(q_head, k_pair), -1e30)
            probs = jnp.exp(scores - stat_ref[:, head : head + 1])
            grad_probs = mm_last(do_head, v_pair)
            grad_scores = (probs * (grad_probs - stat_ref[:, 8 + head : 9 + head])).astype(low)
            grads.append(mm(grad_scores, k_pair))
        grad_query_out[:, cols] = (
            jnp.where(pair_half(T, 0), grads[0], grads[1]) * (1.0 / math.sqrt(HEAD_DIM))
        ).astype(low)


def slot_rows(meta, sums, act_ref, count, step):
    big = meta[0] == 1
    slot_line = lax.broadcasted_iota(jnp.int32, (BLOCKS, W), 0)
    joined = []
    for block in range(count):
        part = sums[4 * block : 4 * block + 4]
        whole = jnp.where(slot_line == 0, jnp.sum(part, axis=0, keepdims=True), 0.0)
        joined.append(jnp.where(big, whole, part))
    first_tile = (meta[1] == 0) & (meta[2] == 0)
    joined.append(jnp.where(first_tile, act_ref[...], 0.0))
    joined.append(jnp.zeros((step - 4 * count - 4, W), full))
    return jnp.concatenate(joined, axis=0).astype(low)


def early_kernel(
    meta,
    activ,
    grad_mlp,
    entry_two,
    grad_inner,
    attended,
    grad_attn,
    small,
    slots,
    act_ref,
    bundle,
):
    half = bundle.shape[1]
    first = bundle.at[meta[2]]
    second = bundle.at[1 - meta[2]]
    first[:FF] = mm_rows(activ[...], grad_mlp[...]).astype(low)
    first[FF : FF + W] = mm_rows(attended[...], grad_attn[...]).astype(low)
    if half > FF + W:
        first[FF + W :] = jnp.zeros((half - FF - W, W), low)
    entry = entry_two[...]
    for slab in range(FF // W):
        second[slab * W : (slab + 1) * W] = mm_rows(
            entry, grad_inner[:, slab * W : (slab + 1) * W]
        ).astype(low)
    second[EARLY_SMALL:EARLY_SLOTS] = small[...].astype(low)
    second[EARLY_SLOTS:] = jnp.zeros((half - EARLY_SLOTS, W), low)
    start = pl.multiple_of(EARLY_SLOTS + meta[3] * EARLY_STEP, 16)
    second[pl.ds(start, EARLY_STEP)] = slot_rows(meta, slots[...], act_ref, 6, EARLY_STEP)


def key_kernel(
    meta,
    qkv_all,
    pay_own,
    pay_row,
    pay_col,
    pay_both,
    grad_query,
    entry_own,
    normed_own,
    inv_own,
    grad_mid,
    mods_ref,
    act_ref,
    patches,
    w_patch,
    w_qkv_low,
    bundle,
    grad_patches,
    gk_ref,
    gv_ref,
):
    big = meta[0] == 1
    allowed = same_image(big, T, ALL)
    tiles = (pay_own, pay_row, pay_col, pay_both)
    packed = jnp.concatenate([tile[:, W:] for tile in tiles], axis=0).astype(full)
    stat = packed + pltpu.roll(packed, 112, 1) + pltpu.roll(packed, 96, 1)
    stat_t = stat.T
    for pair in range(HEADS // 2):
        cols = slice(pair * 2 * HEAD_DIM, (pair + 1) * 2 * HEAD_DIM)
        q_pair = qkv_all[:, cols]
        k_pair = qkv_all[:T, W + cols.start : W + cols.stop] * low(1.0 / math.sqrt(HEAD_DIM))
        v_pair = qkv_all[:T, 2 * W + cols.start : 2 * W + cols.stop]
        do_pair = jnp.concatenate([tile[:, cols] for tile in tiles], axis=0)
        grad_k = []
        grad_v = []
        for half in range(2):
            head = 2 * pair + half
            k_head = jnp.where(pair_half(T, half), k_pair, low(0.0))
            v_head = jnp.where(pair_half(T, half), v_pair, low(0.0))
            scores = jnp.where(allowed, mm_last(k_head, q_pair), -1e30)
            probs = jnp.exp(scores - stat_t[head : head + 1])
            grad_probs = mm_last(v_head, do_pair)
            grad_scores = (probs * (grad_probs - stat_t[8 + head : 9 + head])).astype(low)
            grad_v.append(mm(probs.astype(low), do_pair))
            grad_k.append(mm(grad_scores, q_pair))
        gk_ref[:, cols] = (
            jnp.where(pair_half(T, 0), grad_k[0], grad_k[1]) * (1.0 / math.sqrt(HEAD_DIM))
        ).astype(low)
        gv_ref[:, cols] = jnp.where(pair_half(T, 0), grad_v[0], grad_v[1]).astype(low)
    entry = entry_own[...]
    grad_q = grad_query[...]
    grad_k = gk_ref[...]
    grad_v = gv_ref[...]
    half = bundle.shape[1]
    first = bundle.at[meta[2]]
    second = bundle.at[1 - meta[2]]
    first[:W] = mm_rows(entry, grad_q).astype(low)
    first[W : 2 * W] = mm_rows(entry, grad_k).astype(low)
    if half > 2 * W:
        first[2 * W :] = jnp.zeros((half - 2 * W, W), low)
    second[:W] = mm_rows(entry, grad_v).astype(low)
    grad_entry = (
        mm_last(grad_q, w_qkv_low[:, :W])
        + mm_last(grad_k, w_qkv_low[:, W : 2 * W])
        + mm_last(grad_v, w_qkv_low[:, 2 * W :])
    )
    normed = normed_own[...]
    scale_a = 1.0 + per_token(mods_ref[...], 1)
    grad_in = grad_mid[...] + norm_back(grad_entry * scale_a, normed, inv_own[...])
    grad_patches[...] = mm_last(w_patch[...], grad_in, exact_mode)
    second[LATE_SMALL:LATE_SLOTS] = jnp.concatenate(
        [
            mm(patches[...], grad_in, exact_mode),
            jnp.sum(grad_in, axis=0, keepdims=True),
            jnp.sum(grad_q.astype(full), axis=0, keepdims=True),
            jnp.sum(grad_v.astype(full), axis=0, keepdims=True),
            jnp.zeros((LATE_SLOTS - LATE_SMALL - PATCH - 3, W), full),
        ],
        axis=0,
    ).astype(low)
    second[LATE_SLOTS:] = jnp.zeros((half - LATE_SLOTS, W), low)
    sums = jnp.concatenate([block_sums(grad_entry), block_sums(grad_entry * normed)], axis=0)
    start = pl.multiple_of(LATE_SLOTS + meta[3] * LATE_STEP, 16)
    second[pl.ds(start, LATE_STEP)] = slot_rows(meta, sums, act_ref, 2, LATE_STEP)


def slot_products(region, count, step):
    rows = region.shape[0]
    place = lax.broadcasted_iota(jnp.int32, (rows, W), 0) & (step - 1)
    region_full = region.astype(full)
    acts = jnp.where(place >> 2 == count, region_full, 0.0)
    products = []
    sums = []
    for block in range(count):
        turned = pltpu.roll(acts, rows - 4 * (count - block), 0).astype(low)
        products.append(mm_rows(turned, region))
        sums.append(
            jnp.sum(jnp.where(place >> 2 == block, region_full, 0.0), axis=0, keepdims=True)
        )
    return products, sums


def slot_back(rows, weight_ref, at, block):
    weight = weight_ref[:, at * W : (at + 1) * W]
    high = weight.astype(low)
    rest = (weight - high.astype(full)).astype(low)
    return (mm_last(rows, high) + mm_last(rows, rest))[4 * block : 4 * block + 4]


def unpack_early_kernel(
    groups,
    meta,
    own,
    other,
    w_mod,
    w_fmod,
    g_fc2,
    g_proj,
    g_fc1,
    g_w_out,
    g_b_proj,
    g_b_fc1,
    g_b_fc2,
    g_b_out,
    g_w_mod,
    g_w_fmod,
    b_mod_part,
    g_b_fmod,
    act_part,
    work,
    sem,
):
    even = meta[2] == 0

    def first(lo, hi):
        return jnp.where(even, own[lo:hi], other[lo:hi])

    def second(lo, hi):
        return jnp.where(even, other[lo:hi], own[lo:hi])

    region = second(EARLY_SLOTS, EARLY_SLOTS + EARLY_STEP * groups)
    products, sums = slot_products(region, 6, EARLY_STEP)
    for block in range(4):
        work[:, block * W : (block + 1) * W] = products[block]
    copy = pltpu.make_async_copy(work, g_w_mod.at[:, 2 * W : 6 * W], sem)
    copy.start()
    for block in range(2):
        g_w_fmod[:, block * W : (block + 1) * W] = products[4 + block]
    b_mod_part[...] = jnp.concatenate(sums[:4], axis=1)[0]
    g_b_fmod[...] = jnp.concatenate(sums[4:], axis=1)[0]
    start = pl.multiple_of(EARLY_SLOTS + meta[3] * EARLY_STEP, 16)
    rows = jnp.where(even, other[pl.ds(start, EARLY_STEP)], own[pl.ds(start, EARLY_STEP)])
    total = slot_back(rows, w_mod, 2, 0)
    for block in range(1, 4):
        total = total + slot_back(rows, w_mod, 2 + block, block)
    for block in range(2):
        total = total + slot_back(rows, w_fmod, block, 4 + block)
    act_part[...] = total
    g_fc2[...] = first(0, FF).astype(full)
    g_proj[...] = first(FF, FF + W).astype(full)
    for slab in range(FF // W):
        g_fc1[:, slab * W : (slab + 1) * W] = second(slab * W, (slab + 1) * W).astype(full)
    small = second(EARLY_SMALL, EARLY_SLOTS).astype(full)
    g_w_out[...] = small[:OUTC].T
    at = OUTC
    g_b_proj[...] = small[at : at + 1][0]
    g_b_fc1[...] = jnp.concatenate([small[at + 1 + i : at + 2 + i] for i in range(4)], axis=1)[0]
    g_b_fc2[...] = small[at + 5 : at + 6][0]
    g_b_out[...] = small[at + 6 : at + 7, :OUTC][0]
    copy.wait()


def unpack_late_kernel(
    groups,
    meta,
    own,
    other,
    cond,
    act_part,
    b_mod_part,
    w_mod_front,
    w_mod_in,
    g_w_mod,
    g_cond,
    g_w_patch,
    g_b_patch,
    g_b_mod,
    g_w_qkv,
    g_b_query,
    g_b_value,
    work,
    sem,
):
    even = meta[2] == 0

    def first(lo, hi):
        return jnp.where(even, own[lo:hi], other[lo:hi])

    def second(lo, hi):
        return jnp.where(even, other[lo:hi], own[lo:hi])

    region = second(LATE_SLOTS, LATE_SLOTS + LATE_STEP * groups)
    products, sums = slot_products(region, 2, LATE_STEP)
    for block in range(2):
        work[:, block * W : (block + 1) * W] = products[block]
    copy = pltpu.make_async_copy(work, g_w_mod.at[:, : 2 * W], sem)
    copy.start()
    g_b_mod[...] = jnp.concatenate(sums + [row_of(b_mod_part)], axis=1)[0]
    start = pl.multiple_of(LATE_SLOTS + meta[3] * LATE_STEP, 16)
    rows = jnp.where(even, other[pl.ds(start, LATE_STEP)], own[pl.ds(start, LATE_STEP)])
    total = act_part[...]
    for block in range(2):
        total = total + slot_back(rows, w_mod_front, block, block)
    value = cond[...]
    gate = 1.0 / (1.0 + jnp.exp(-value))
    g_cond[...] = total * gate * (1.0 + value * (1.0 - gate))
    for slab in range(2):
        g_w_qkv[:, slab * W : (slab + 1) * W] = first(slab * W, (slab + 1) * W).astype(full)
    g_w_qkv[:, 2 * W :] = second(0, W).astype(full)
    small = second(LATE_SMALL, LATE_SLOTS).astype(full)
    g_w_patch[...] = small[:PATCH]
    g_b_patch[...] = small[PATCH : PATCH + 1][0]
    g_b_query[...] = small[PATCH + 1 : PATCH + 2][0]
    g_b_value[...] = small[PATCH + 2 : PATCH + 3][0]
    copy.wait()


def bit_swap(array, axis_name, bit):
    size = lax.axis_size(axis_name)
    return lax.ppermute(array, axis_name, [(i, i ^ (1 << bit)) for i in range(size)])


def bit_here(axis_name, bit):
    return (lax.axis_index(axis_name) >> bit) & 1


def batch_bits():
    size = lax.axis_size("batch")
    assert size & (size - 1) == 0
    return size.bit_length() - 1


def two_way_swap(array, pair):
    sizes = [lax.axis_size(name) for name in ("batch", "row", "col")]
    moves = []
    for group in range(sizes[0]):
        for row in range(sizes[1]):
            for col in range(sizes[2]):
                place = {"batch": group, "row": row}
                axis_name, bit = pair[col]
                place[axis_name] ^= 1 << bit
                moves.append(
                    (
                        (group * sizes[1] + row) * sizes[2] + col,
                        (place["batch"] * sizes[1] + place["row"]) * sizes[2] + col,
                    )
                )
    return lax.ppermute(array, ("batch", "row", "col"), moves)


def sum_halves(stack, orders):
    core = lax.axis_index("col")
    got = bit_swap(stack[1], "col", 0)
    part = (stack[0].astype(full) + got.astype(full)).astype(low)
    pairs = list(zip(*orders))
    heres = [jnp.where(core == 0, bit_here(*pair[0]), bit_here(*pair[1])) for pair in pairs]
    for pair, here in zip(pairs, heres):
        half = part.shape[0] // 2
        keep = lax.dynamic_slice_in_dim(part, here * half, half, 0)
        send = lax.dynamic_slice_in_dim(part, (1 - here) * half, half, 0)
        got = two_way_swap(send, pair)
        part = (keep.astype(full) + got.astype(full)).astype(low)
    for pair, here in zip(reversed(pairs), reversed(heres)):
        got = two_way_swap(part, pair)
        part = jnp.concatenate(
            [jnp.where(here == 0, part, got), jnp.where(here == 0, got, part)], axis=0
        )
    return part, bit_swap(part, "col", 0)


def link_orders():
    bits = [("batch", bit) for bit in range(batch_bits())]
    row = [("row", 0)]
    early = (bits[:1] + row + bits[1:], bits[1:2] + bits[:1] + row + bits[2:])
    late = (row + bits, bits[:2] + row + bits[2:])
    return early, late


def cost(microseconds):
    return pl.CostEstimate(
        flops=int(microseconds * 1e9), bytes_accessed=0, transcendentals=0
    )


def half_rows(needed, devices):
    unit = 8 * devices // 2
    return -(-needed // unit) * unit


def shaped(*pairs):
    return [jax.ShapeDtypeStruct(shape, kind) for shape, kind in pairs]


vmem = pl.BlockSpec(memory_space=pltpu.VMEM)
smem = pl.BlockSpec(memory_space=pltpu.SMEM)
hbm = pl.BlockSpec(memory_space=pl.ANY)


def position_table():
    quarter = W // 4
    rates = 1.0 / jnp.power(10000.0, jnp.arange(quarter, dtype=full) / quarter)
    angle = jnp.arange(32, dtype=full)[:, None] * rates[None, :]
    waves = jnp.concatenate([jnp.sin(angle), jnp.cos(angle)], axis=1)
    return jnp.concatenate(
        [jnp.pad(waves, ((0, 0), (0, W // 2))), jnp.pad(waves, ((0, 0), (W // 2, 0)))], axis=0
    )


def tile_copies(array):
    by_row = bit_swap(array, "row", 0)
    by_col = bit_swap(array, "col", 0)
    return array, by_row, by_col, bit_swap(by_row, "col", 0)


def body(
    patches,
    cond,
    image_lengths,
    cotangent,
    w_patch,
    b_patch,
    w_mod,
    b_mod,
    w_qkv,
    b_query,
    b_value,
    w_proj,
    b_proj,
    w_fc1,
    b_fc1,
    w_fc2,
    b_fc2,
    w_fmod,
    b_fmod,
    w_out,
    b_out,
):
    groups = lax.axis_size("batch")
    devices = groups * lax.axis_size("row") * lax.axis_size("col")
    patch_cols = patches[0, 0, 0]
    patch_tiles = tile_copies(patch_cols)
    big = image_lengths[0, 0, 0] == BIG_LEN
    group = lax.axis_index("batch")
    meta = jnp.stack(
        [big.astype(jnp.int32), lax.axis_index("row"), lax.axis_index("col"), group]
    ).astype(jnp.int32)
    act = jax.nn.silu(cond[0])
    mods = jnp.concatenate(
        [
            jnp.dot(act, w_mod, precision=exact_mode) + b_mod,
            jnp.dot(act, w_fmod, precision=exact_mode) + b_fmod,
        ],
        axis=1,
    )
    mods = jnp.where(big, mods[:1], mods)
    (
        result,
        payload,
        qkv_all,
        entry_own,
        normed_own,
        inv_own,
        attended,
        grad_attn,
        grad_mid,
        activ,
        grad_mlp,
        entry_two,
        grad_inner,
        small,
        slots,
        w_qkv_low,
        stat,
    ) = pl.pallas_call(
        lambda *refs: front_kernel(
            *refs[:37], *refs[38:44], refs[37], *refs[44:]
        ),
        name="front",
        in_specs=[smem] + [vmem] * 16 + [hbm] * 4,
        cost_estimate=cost(16),
        out_specs=[vmem] * 17,
        out_shape=shaped(
            ((OUTC, T), full),
            ((T, W + 128), low),
            ((ALL, 3 * W), low),
            ((T, W), low),
            ((T, W), full),
            ((T, 1), full),
            ((T, W), low),
            ((T, W), low),
            ((T, W), full),
            ((T, FF), low),
            ((T, W), low),
            ((T, W), low),
            ((T, FF), low),
            ((48, W), full),
            ((24, W), full),
            ((W, 3 * W), low),
            ((T, 128), full),
        ),
        scratch_shapes=[
            pltpu.VMEM((W, 3 * W), full),
            pltpu.VMEM((W, W), full),
            pltpu.VMEM((W, FF), full),
            pltpu.VMEM((FF, W), full),
            pltpu.VMEM((ALL, W), low),
            pltpu.VMEM((T, W), full),
            pltpu.VMEM((T, FF), full),
            pltpu.SemaphoreType.DMA((4,)),
        ],
    )(
        meta,
        *patch_tiles,
        cotangent[0, 0, 0],
        mods,
        w_patch,
        position_table(),
        b_patch,
        b_query,
        b_value,
        b_proj,
        b_fc1,
        b_fc2,
        w_out,
        b_out,
        w_qkv,
        w_proj,
        w_fc1,
        w_fc2,
    )
    payload_tiles = tile_copies(payload)
    early_half = half_rows(max(FF + W, EARLY_SLOTS + groups * EARLY_STEP), devices)
    early = pl.pallas_call(
        early_kernel,
        name="early_side",
        in_specs=[smem] + [vmem] * 9,
        out_specs=vmem,
        out_shape=jax.ShapeDtypeStruct((2, early_half, W), low),
        cost_estimate=cost(3),
    )(
        meta,
        activ,
        grad_mlp,
        entry_two,
        grad_inner,
        attended,
        grad_attn,
        small,
        slots,
        act,
    )
    early_orders, late_orders = link_orders()
    early_own, early_other = sum_halves(early, early_orders)
    grad_query = pl.pallas_call(
        query_kernel,
        name="query_side",
        in_specs=[smem] + [vmem] * 3,
        out_specs=vmem,
        out_shape=jax.ShapeDtypeStruct((T, W), low),
        cost_estimate=cost(5),
    )(meta, qkv_all, payload, stat)
    late_half = half_rows(max(2 * W, LATE_SLOTS + groups * LATE_STEP), devices)
    late, grad_patch_cols = pl.pallas_call(
        key_kernel,
        name="key_side",
        in_specs=[smem] + [vmem] * 15,
        out_specs=[vmem] * 2,
        out_shape=shaped(((2, late_half, W), low), ((PATCH, T), full)),
        scratch_shapes=[pltpu.VMEM((T, W), low), pltpu.VMEM((T, W), low)],
        cost_estimate=cost(9),
    )(
        meta,
        qkv_all,
        *payload_tiles,
        grad_query,
        entry_own,
        normed_own,
        inv_own,
        grad_mid,
        mods,
        act,
        patch_cols,
        w_patch,
        w_qkv_low,
    )
    late_own, late_other = sum_halves(late, late_orders)
    (
        g_fc2,
        g_proj,
        g_fc1,
        g_w_out,
        g_b_proj,
        g_b_fc1,
        g_b_fc2,
        g_b_out,
        g_w_mod,
        g_w_fmod,
        b_mod_part,
        g_b_fmod,
        act_part,
    ) = pl.pallas_call(
        lambda *refs: unpack_early_kernel(groups, *refs),
        name="unpack_early",
        in_specs=[smem] + [vmem] * 4,
        out_specs=[vmem] * 8 + [hbm] + [vmem] * 4,
        out_shape=shaped(
            ((FF, W), full),
            ((W, W), full),
            ((W, FF), full),
            ((W, OUTC), full),
            ((W,), full),
            ((FF,), full),
            ((W,), full),
            ((OUTC,), full),
            ((W, 6 * W), full),
            ((W, 2 * W), full),
            ((4 * W,), full),
            ((2 * W,), full),
            ((4, W), full),
        ),
        scratch_shapes=[pltpu.VMEM((W, 4 * W), full), pltpu.SemaphoreType.DMA(())],
        cost_estimate=cost(8),
    )(meta, early_own, early_other, w_mod, w_fmod)
    (
        g_w_mod,
        g_cond,
        g_w_patch,
        g_b_patch,
        g_b_mod,
        g_w_qkv,
        g_b_query,
        g_b_value,
    ) = pl.pallas_call(
        lambda *refs: unpack_late_kernel(groups, *refs),
        name="unpack_late",
        in_specs=[smem] + [vmem] * 6 + [hbm],
        out_specs=[hbm] + [vmem] * 7,
        out_shape=shaped(
            ((W, 6 * W), full),
            ((4, W), full),
            ((PATCH, W), full),
            ((W,), full),
            ((6 * W,), full),
            ((W, 3 * W), full),
            ((W,), full),
            ((W,), full),
        ),
        scratch_shapes=[pltpu.VMEM((W, 2 * W), full), pltpu.SemaphoreType.DMA(())],
        input_output_aliases={7: 0},
        cost_estimate=cost(5),
    )(
        meta,
        late_own,
        late_other,
        cond[0],
        act_part,
        b_mod_part,
        w_mod[:, : 2 * W],
        g_w_mod,
    )
    grad_cond = g_cond[None]
    summed = (
        g_w_patch,
        g_b_patch,
        g_w_mod,
        g_b_mod,
        g_w_qkv,
        g_b_query,
        g_b_value,
        g_proj,
        g_b_proj,
        g_fc1,
        g_b_fc1,
        g_fc2,
        g_b_fc2,
        g_w_fmod,
        g_b_fmod,
        g_w_out,
        g_b_out,
    )
    return (result[None, None, None], grad_patch_cols[None, None, None], grad_cond) + tuple(
        summed
    )


def solution(mesh):
    placed = (
        P("batch", "row", "col", None, None),
        P("batch", None, None),
        P("batch", None, None),
        P("batch", "row", "col", None, None),
        P(),
        P(),
        P(),
        P(),
        P(),
        P(),
        P(),
        P(),
        P(),
        P(),
        P(),
        P(),
        P(),
        P(),
        P(),
        P(),
        P(),
    )
    return jax.shard_map(
        body,
        mesh=mesh,
        in_specs=placed,
        out_specs=(
            P("batch", "row", "col", None, None),
            P("batch", "row", "col", None, None),
            P("batch", None, None),
            P(),
            P(),
            P(),
            P(),
            P(),
            P(),
            P(),
            P(),
            P(),
            P(),
            P(),
            P(),
            P(),
            P(),
            P(),
            P(),
            P(),
        ),
        check_vma=False,
    )
```
